128 devices in a mesh: ctx: 32 (over y, x, z_lo), batch: 4 (over z_hi, core).
Axes of the slice: x: 4, y: 4, z: 4 (z_hi: 2, z_lo: 2; z = z_hi * 2 + z_lo), core: 2. Of those that a mesh axis runs over, the one named last changes fastest.
Arguments:
- queries: bfloat16 [4, 8192, 2048], P('batch', 'ctx'), may hold values from -120 to 120
- keys: bfloat16 [4, 8192, 512], P('batch', 'ctx'), may hold values from -6 to 6
- values: bfloat16 [4, 8192, 512], P('batch', 'ctx'), may hold values from -6 to 6
- tau: float32 [16], replicated, may hold values from 0.5 to 2
- out_grad: bfloat16 [4, 8192, 2048], P('batch', 'ctx'), may hold values from -18 to 18
- key_blocks: int32 [4, 64, 13], replicated, may hold values from 0 to 63, as said below
Outputs:
- attended: bfloat16 [4, 8192, 2048], P('batch', 'ctx')
- query_grad: bfloat16 [4, 8192, 2048], P('batch', 'ctx')
- key_grad: bfloat16 [4, 8192, 512], P('batch', 'ctx')
- value_grad: bfloat16 [4, 8192, 512], P('batch', 'ctx')
- tau_grad: float32 [16], replicated
The draws below stay inside these ranges and needn't reach their ends.
Inputs may be any that keep to these rules, and one draw needn't show every extreme that they name: `key_blocks`: row a of head group g lists a - 1, a, a + 1, then a + m s and a - m s for m = 1 to 5, all modulo 64, with a stride s of 2 or 3 drawn for each group and row.
All inputs are finite; a program needn't handle non-finite values.
Results may differ from the reference program's by a relative error of at most 0.0051.
Values may be sent and summed in bfloat16 or wider, within the bound.
A program may use at most 192 MiB of HBM per device.

```python
import math
import jax
import jax.numpy as jnp
from jax import lax

HEADS = 16
KV_HEADS = 4
HD = 128
BLOCK = 128
KMAX = 13
QPG = 4
BATCHES = 4
SEQ = 8192
NB = 64


def paired(key):
    base_keys = jnp.clip(jax.random.normal(jax.random.fold_in(key, 11), (BATCHES, SEQ, KV_HEADS, HD), jnp.float32), -6.0, 6.0)
    base_queries = jnp.clip(jax.random.normal(jax.random.fold_in(key, 12), (BATCHES, SEQ, KV_HEADS, QPG, HD), jnp.float32), -6.0, 6.0)
    return (base_keys, base_queries)


def draw_keys(key, part):
    base_keys, base_queries = paired(key)
    return base_keys.reshape(BATCHES, SEQ, KV_HEADS * HD).astype(jnp.bfloat16)


def draw_queries(key, part):
    base_keys, base_queries = paired(key)
    return base_queries.reshape(BATCHES, SEQ, HEADS * HD).astype(jnp.bfloat16)


def draw_out_grad(key, part):
    ramp = 1.0 + 2.0 * jnp.arange(SEQ, dtype=jnp.float32) / SEQ
    noise = jnp.clip(jax.random.normal(jax.random.fold_in(key, 22), (BATCHES, SEQ, HEADS * HD), jnp.float32), -6.0, 6.0)
    return (noise * ramp[None, :, None]).astype(jnp.bfloat16)


def draw_key_blocks(key, part):
    stride = jax.random.randint(jax.random.fold_in(key, 31), (KV_HEADS, NB, 1), 2, 4)
    rows = jnp.arange(NB, dtype=jnp.int32)[None, :, None]
    band = jnp.array([-1, 0, 1], jnp.int32)[None, None, :] + jnp.zeros((KV_HEADS, NB, 1), jnp.int32)
    multiples = jnp.arange(1, (KMAX - 3) // 2 + 1, dtype=jnp.int32)[None, None, :]
    offsets = jnp.concatenate([band, stride * multiples, -stride * multiples], axis=2)
    return ((rows + offsets) % NB).astype(jnp.int32)


def block_scale(own_key, shape, shards, least, high):
    def one(dim, blocks):
        steps = jax.random.uniform(jax.random.fold_in(jax.random.fold_in(own_key, 6), dim), (blocks,), jnp.float32, least / len(shards), high / len(shards))
        return jnp.repeat(jnp.exp(steps), shape[dim] // blocks).reshape((-1,) + (1,) * (len(shape) - dim - 1))

    level = one(*shards[0])
    for cut in shards[1:]:
        level = level * one(*cut)
    return level


def centred(rng, extent, deviation, bound, pieces=(), held_as=jnp.bfloat16):
    gain = block_scale(rng, extent, pieces, -0.22, 0.18) if pieces else 1.0
    values = jax.random.normal(rng, extent, jnp.float32) * deviation * gain
    return jnp.minimum(jnp.maximum(values, -bound), bound).astype(held_as)


def setup_inputs(seed: int = 0) -> dict:
    splits = jax.random.split(jax.random.key(seed), 7)
    queries = draw_queries(jax.random.fold_in(splits[6], 71), 0)
    keys = draw_keys(jax.random.fold_in(splits[6], 71), 0)
    values = centred(splits[2], (BATCHES, SEQ, KV_HEADS * HD), 1.0, 6.0, ((0, 4), (1, 32)))
    tau = jnp.clip(jnp.exp(jax.random.uniform(splits[3], (HEADS,), jnp.float32, math.log(0.5), math.log(2.0))), 0.5, 2.0)
    out_grad = draw_out_grad(jax.random.fold_in(splits[6], 71), 0)
    key_blocks = draw_key_blocks(jax.random.fold_in(splits[6], 71), 0)
    return {"queries": queries, "keys": keys, "values": values, "tau": tau, "out_grad": out_grad, "key_blocks": key_blocks}


highest = lax.Precision.HIGHEST

def low_round(array):
    return lax.optimization_barrier(array.astype(jnp.bfloat16)).astype(jnp.float32)

def one_group(query_block, grad_block, key_group, value_group, listed, scale_row):
    key_rows = jnp.take(key_group, listed, axis=0).reshape(KMAX * BLOCK, HD).astype(jnp.float32)
    value_rows = jnp.take(value_group, listed, axis=0).reshape(KMAX * BLOCK, HD).astype(jnp.float32)
    query_rows = query_block.astype(jnp.float32)
    grad_rows = grad_block.astype(jnp.float32)
    raw_scores = jnp.einsum('qhd,kd->hqk', query_rows, key_rows, precision=highest)
    weights = jax.nn.softmax(raw_scores * scale_row[:, None, None], axis=-1)
    probs_low = low_round(weights)
    result = jnp.einsum('hqk,kd->qhd', probs_low, value_rows, precision=highest)
    row_dot = lax.optimization_barrier(jnp.sum(grad_rows * result, axis=-1))
    dweights = jnp.einsum('qhd,kd->hqk', grad_rows, value_rows, precision=highest)
    dscores = weights * (dweights - row_dot.T[:, :, None])
    scale_part = lax.optimization_barrier(jnp.sum(dscores * raw_scores, axis=(1, 2))) / math.sqrt(HD)
    scaled = low_round(dscores * scale_row[:, None, None])
    query_part = jnp.einsum('hqk,kd->qhd', scaled, key_rows, precision=highest)
    key_part = jnp.einsum('hqk,qhd->kd', scaled, query_rows, precision=highest)
    value_part = jnp.einsum('hqk,qhd->kd', probs_low, grad_rows, precision=highest)
    return (result, query_part, key_part.reshape(KMAX, BLOCK, HD), value_part.reshape(KMAX, BLOCK, HD), scale_part)

def reference(queries, keys, values, tau, out_grad, key_blocks):
    nblocks = SEQ // BLOCK
    scale_all = (tau.astype(jnp.float32) / math.sqrt(HD)).reshape(KV_HEADS, QPG)
    group_ids = jnp.arange(KV_HEADS, dtype=jnp.int32)
    outputs = []
    query_grads = []
    key_grads = []
    value_grads = []
    scale_total = jnp.zeros((KV_HEADS, QPG), jnp.float32)
    for seq_index in range(BATCHES):
        query_seq = queries[seq_index].reshape(nblocks, BLOCK, KV_HEADS, QPG, HD)
        grad_seq = out_grad[seq_index].reshape(nblocks, BLOCK, KV_HEADS, QPG, HD)
        key_seq = keys[seq_index].reshape(nblocks, BLOCK, KV_HEADS, HD).transpose(2, 0, 1, 3)
        value_seq = values[seq_index].reshape(nblocks, BLOCK, KV_HEADS, HD).transpose(2, 0, 1, 3)

        def step_fn(state_in, index):
            key_acc, value_acc, scale_acc = state_in
            query_block = query_seq[index].transpose(1, 0, 2, 3)
            grad_block = grad_seq[index].transpose(1, 0, 2, 3)
            listed = key_blocks[:, index, :].astype(jnp.int32)
            result, query_part, key_part, value_part, scale_part = jax.vmap(one_group)(query_block, grad_block, key_seq, value_seq, listed, scale_all)
            key_acc = key_acc.at[group_ids[:, None], listed].add(key_part)
            value_acc = value_acc.at[group_ids[:, None], listed].add(value_part)
            return ((key_acc, value_acc, scale_acc + scale_part), (result, query_part))
        zeros = jnp.zeros((KV_HEADS, nblocks, BLOCK, HD), jnp.float32)
        start = (zeros, zeros, jnp.zeros((KV_HEADS, QPG), jnp.float32))
        (key_acc, value_acc, scale_acc), (results, query_parts) = lax.scan(step_fn, start, jnp.arange(nblocks, dtype=jnp.int32))
        outputs.append(results.transpose(0, 2, 1, 3, 4).reshape(SEQ, HEADS * HD).astype(jnp.bfloat16))
        query_grads.append(query_parts.transpose(0, 2, 1, 3, 4).reshape(SEQ, HEADS * HD).astype(jnp.bfloat16))
        key_grads.append(key_acc.transpose(1, 2, 0, 3).reshape(SEQ, KV_HEADS * HD).astype(jnp.bfloat16))
        value_grads.append(value_acc.transpose(1, 2, 0, 3).reshape(SEQ, KV_HEADS * HD).astype(jnp.bfloat16))
        scale_total = scale_total + scale_acc
    tau_grad = scale_total.reshape(HEADS) / math.sqrt(BATCHES * SEQ)
    return (jnp.stack(outputs), jnp.stack(query_grads), jnp.stack(key_grads), jnp.stack(value_grads), tau_grad)
```

```python
import math

import jax
import jax.numpy as jnp
from jax import lax
from jax.experimental import pallas as pl
from jax.experimental.pallas import tpu as pltpu
from jax.sharding import PartitionSpec as P

HEADS = 16
GROUPS = 4
PER = HEADS // GROUPS
HD = 128
BLOCK = 128
WIDE = PER * HD
NY, NX, NZ = 4, 4, 2
OWN = 2
ROWS = NX * OWN
HALF = NX * OWN
PLANE = NZ * HALF
WINDOW = 3 * PLANE
f32 = jnp.float32
bf16 = jnp.bfloat16


def index_of(y, x, z):
    return (y % NY) * (NX * NZ) + (x % NX) * NZ + z % NZ


def shifted(value, dy, dx, dz):
    route = [
        (index_of(y, x, z), index_of(y + dy, x + dx, z + dz))
        for y in range(NY)
        for x in range(NX)
        for z in range(NZ)
    ]
    return lax.ppermute(value, "ctx", route)


def dot(a, b, ca, cb):
    return lax.dot_general(a, b, (((ca,), (cb,)), ((), ())), preferred_element_type=f32)


def attention_kernel(listed, table, *refs):
    qs = refs[0:NX]
    gs = refs[NX : 2 * NX]
    bundles = refs[2 * NX : 2 * NX + 6]
    scale_ref = refs[2 * NX + 6]
    outs = refs[2 * NX + 7 :]
    ods = outs[0:NX]
    fars = outs[NX : NX + 4]
    nears = outs[NX + 4 : NX + 6]
    tau_ref = outs[NX + 6]
    q_all, g_all, kw, vw, s_scr, e_scr, dk_acc, dv_acc, od, in_sem, od_sem = outs[NX + 7 :]
    r = pl.program_id(0)

    @pl.when(r == 0)
    def _():
        copies = []
        for d in range(NX):
            copies.append((qs[d], q_all.at[pl.ds(d * OWN * BLOCK, OWN * BLOCK)]))
            copies.append((gs[d], g_all.at[pl.ds(d * OWN * BLOCK, OWN * BLOCK)]))
        for i in range(6):
            copies.append((bundles[i].at[0], kw.at[pl.ds(i * HALF, HALF)]))
            copies.append((bundles[i].at[1], vw.at[pl.ds(i * HALF, HALF)]))
        started = []
        for i, (src, dst) in enumerate(copies):
            copy = pltpu.make_async_copy(src, dst, in_sem.at[i])
            copy.start()
            started.append(copy)
        dk_acc[...] = jnp.zeros_like(dk_acc)
        dv_acc[...] = jnp.zeros_like(dv_acc)
        tau_ref[...] = jnp.zeros_like(tau_ref)
        for copy in started:
            copy.wait()

    rows = pl.ds(pl.multiple_of(r * BLOCK, BLOCK), BLOCK)
    q = jnp.concatenate([q_all[rows, h * HD : (h + 1) * HD] for h in range(PER)], 0)
    g = jnp.concatenate([g_all[rows, h * HD : (h + 1) * HD] for h in range(PER)], 0)
    scale = scale_ref[0:1, :]
    high = None
    for k in range(listed):
        s = dot(kw[table[r * listed + k]], q, 1, 1)
        s_scr[k] = s
        top = s.reshape(16, 8, WIDE).max(0)
        high = top if high is None else jnp.maximum(high, top)
    high = high.max(0, keepdims=True)
    total = jnp.zeros((8, WIDE), f32)
    for k in range(listed):
        e = jnp.exp((s_scr[k] - high) * scale)
        e_scr[k] = e
        total = total + e.reshape(16, 8, WIDE).sum(0)
    inverse = 1.0 / total.sum(0, keepdims=True)
    o = None
    for k in range(listed):
        slot = table[r * listed + k]
        p = (e_scr[k] * inverse).astype(bf16)
        dv_acc[slot] += dot(p, g, 1, 0)
        part = dot(p, vw[slot], 0, 0)
        o = part if o is None else o + part
    for h in range(PER):
        od[r, 0, :, h * HD : (h + 1) * HD] = o[h * BLOCK : (h + 1) * BLOCK].astype(bf16)
    row_dot = (g.astype(f32) * o).sum(-1, keepdims=True)
    row_dot = jnp.broadcast_to(row_dot, (WIDE, HD)).T[0:1]
    tau = jnp.zeros((8, WIDE), f32)
    dq = None
    factor = inverse * scale
    for k in range(listed):
        slot = table[r * listed + k]
        t = e_scr[k] * (dot(vw[slot], g, 1, 1) - row_dot)
        tau = tau + (t * s_scr[k]).reshape(16, 8, WIDE).sum(0)
        ds = (t * factor).astype(bf16)
        dk_acc[slot] += dot(ds, q, 1, 0)
        part = dot(ds, kw[slot], 0, 0)
        dq = part if dq is None else dq + part
    for h in range(PER):
        od[r, 1, :, h * HD : (h + 1) * HD] = dq[h * BLOCK : (h + 1) * BLOCK].astype(bf16)
    tau_ref[...] += tau * inverse

    def sent(row, d):
        return pltpu.make_async_copy(od.at[row], ods[d].at[row - d * OWN], od_sem.at[row])

    for row in range(ROWS):

        @pl.when(r == row)
        def _(row=row):
            sent(row, row // OWN).start()

    @pl.when(r == ROWS - 1)
    def _():
        for kv, acc in enumerate((dk_acc, dv_acc)):
            for i in range(2):
                nears[i][kv] = acc[pl.ds(i * HALF, HALF)]
            for i in range(4):
                fars[i][kv] = acc[pl.ds(PLANE + i * HALF, HALF)].astype(bf16)
        for row in range(ROWS):
            sent(row, row // OWN).wait()


def attention(table, qs, gs, bundles, scale):
    listed = table.shape[0] // ROWS
    anywhere = pl.BlockSpec(memory_space=pl.ANY)
    half = (2, HALF, BLOCK, HD)

    def whole(shape):
        return pl.BlockSpec(shape, lambda r, *_: (0,) * len(shape))

    out_shape = (
        [jax.ShapeDtypeStruct((OWN, 2, BLOCK, WIDE), bf16)] * NX
        + [jax.ShapeDtypeStruct(half, bf16)] * 4
        + [jax.ShapeDtypeStruct(half, f32)] * 2
        + [jax.ShapeDtypeStruct((8, WIDE), f32)]
    )
    flops = ROWS * listed * BLOCK * WIDE * HD * 12
    outs = pl.pallas_call(
        lambda *refs: attention_kernel(listed, *refs),
        name="attention",
        out_shape=out_shape,
        grid_spec=pltpu.PrefetchScalarGridSpec(
            num_scalar_prefetch=1,
            grid=(ROWS,),
            in_specs=[anywhere] * (2 * NX + 6) + [whole((8, WIDE))],
            out_specs=[anywhere] * NX + [whole(half)] * 6 + [whole((8, WIDE))],
            scratch_shapes=[
                pltpu.VMEM((ROWS * BLOCK, WIDE), bf16),
                pltpu.VMEM((ROWS * BLOCK, WIDE), bf16),
                pltpu.VMEM((WINDOW, BLOCK, HD), bf16),
                pltpu.VMEM((WINDOW, BLOCK, HD), bf16),
                pltpu.VMEM((listed, BLOCK, WIDE), f32),
                pltpu.VMEM((listed, BLOCK, WIDE), f32),
                pltpu.VMEM((WINDOW, BLOCK, HD), f32),
                pltpu.VMEM((WINDOW, BLOCK, HD), f32),
                pltpu.VMEM((ROWS, 2, BLOCK, WIDE), bf16),
                pltpu.SemaphoreType.DMA((2 * NX + 12,)),
                pltpu.SemaphoreType.DMA((ROWS,)),
            ],
        ),
        compiler_params=pltpu.CompilerParams(vmem_limit_bytes=56 << 20),
        cost_estimate=pl.CostEstimate(
            flops=flops, bytes_accessed=12 << 20, transcendentals=ROWS * listed * BLOCK * WIDE
        ),
    )(table, *qs, *gs, *bundles, scale)
    return outs[:NX], outs[NX : NX + 4], outs[NX + 4 : NX + 6], outs[NX + 6]


def columns(array, place, width):
    return lax.dynamic_slice_in_dim(array, place * width, width, 1)


def side_by_side(pieces, x, width):
    rows = pieces[0].shape[0]
    whole = jnp.zeros((rows, NX * width), pieces[0].dtype)
    for d in range(NX):
        whole = lax.dynamic_update_slice(whole, pieces[d], (0, (x + d) % NX * width))
    return whole


def body(queries, keys, values, tau, out_grad, key_blocks):
    me = lax.axis_index("ctx")
    y, x, z = me // (NX * NZ), me // NZ % NX, me % NZ
    tokens = queries.shape[1]
    listed = key_blocks.shape[2]
    queries, keys, values, out_grad = queries[0], keys[0], values[0], out_grad[0]

    pieces = []
    for d in range(NX):
        to = (x + d) % NX
        pair = jnp.stack([columns(keys, to, HD), columns(values, to, HD)])
        pieces.append(pair if d == 0 else shifted(pair, 0, d, 0))
    own = jnp.stack(pieces, 1).reshape(2, HALF, BLOCK, HD)
    own, queries, out_grad = lax.optimization_barrier((own, queries, out_grad))

    below = shifted(own, 1, 0, 0)
    above = shifted(own, -1, 0, 0)
    other = shifted(own, 0, 0, 1)
    below_other = shifted(other, 1, 0, 0)
    above_other = shifted(other, -1, 0, 0)
    bundles = [own, other, below, below_other, above, above_other]

    qs, gs = [], []
    for d in range(NX):
        to = (x + d) % NX
        q, g = columns(queries, to, WIDE), columns(out_grad, to, WIDE)
        qs.append(q if d == 0 else shifted(q, 0, d, 0))
        gs.append(g if d == 0 else shifted(g, 0, d, 0))

    lists = lax.dynamic_index_in_dim(key_blocks, x, 0, keepdims=False)
    lists = lists.reshape(NY, NX, NZ, OWN, listed)
    lists = lax.dynamic_index_in_dim(lists, y, 0, keepdims=False)
    lists = lax.dynamic_index_in_dim(lists, z, 1, keepdims=False)
    lists = lists[(x - jnp.arange(NX)) % NX].reshape(-1)
    plane = (lists // 16 - y + 4) % NY
    plane = jnp.where(plane == 0, 0, jnp.where(plane == 3, 1, 2))
    far = jnp.where(lists // OWN % NZ == z, 0, 1)
    table = plane * PLANE + far * HALF + (x - lists // 4 + 64) % NX * OWN + lists % OWN

    mine = lax.dynamic_index_in_dim(tau.reshape(GROUPS, PER), x, 0, keepdims=False)
    scale = jnp.broadcast_to(jnp.repeat(mine / math.sqrt(HD), BLOCK)[None], (8, WIDE))

    ods, fars, nears, tau_part = attention(table.astype(jnp.int32), qs, gs, bundles, scale)

    below_own, below_far, above_own, above_far = fars
    far_sum = (
        nears[1] + shifted(below_far, -1, 0, 0).astype(f32) + shifted(above_far, 1, 0, 0).astype(f32)
    )
    from_other = shifted(far_sum.astype(bf16), 0, 0, 1)
    own_sum = (
        nears[0]
        + shifted(below_own, -1, 0, 0).astype(f32)
        + shifted(above_own, 1, 0, 0).astype(f32)
        + from_other.astype(f32)
    )
    done = own_sum.astype(bf16).reshape(2, NX, OWN * BLOCK, HD)
    kv_pieces = []
    od_pieces = []
    for d in range(NX):
        piece = done[:, d]
        kv_pieces.append(piece if d == 0 else shifted(piece, 0, -d, 0))
        piece = ods[d]
        od_pieces.append(piece if d == 0 else shifted(piece, 0, -d, 0))
    key_grad = side_by_side([p[0] for p in kv_pieces], x, HD)[None]
    value_grad = side_by_side([p[1] for p in kv_pieces], x, HD)[None]
    attended = side_by_side([p[:, 0].reshape(tokens, WIDE) for p in od_pieces], x, WIDE)[None]
    query_grad = side_by_side([p[:, 1].reshape(tokens, WIDE) for p in od_pieces], x, WIDE)[None]

    heads = tau_part.reshape(8, PER, BLOCK).sum((0, 2)) / math.sqrt(HD)
    placed = lax.dynamic_update_slice(jnp.zeros((GROUPS, PER), f32), heads[None], (x, 0))
    scale_total = lax.psum(placed, ("ctx", "batch"))
    count = lax.axis_size("batch") * lax.axis_size("ctx") * tokens
    tau_grad = scale_total.reshape(HEADS) / math.sqrt(count)
    return (attended, query_grad, key_grad, value_grad, tau_grad)


def solution(mesh):
    sharded = P("batch", "ctx", None)
    return jax.shard_map(
        body,
        mesh=mesh,
        in_specs=(sharded, sharded, sharded, P(), sharded, P()),
        out_specs=(sharded, sharded, sharded, sharded, P()),
        check_vma=False,
    )
```

```python
import math

import jax
import jax.numpy as jnp
from jax import lax
from jax.experimental import pallas as pl
from jax.experimental.pallas import tpu as pltpu
from jax.sharding import PartitionSpec as P

HEADS = 16
GROUPS = 4
PER = HEADS // GROUPS
HD = 128
BLOCK = 128
BLOCKS = 64
WIDE = PER * HD
NY, NX, NZ = 4, 4, 2
OWN = 2
ROWS = NX * OWN
HALF = NX * OWN
PLANE = NZ * HALF
WINDOW = 3 * PLANE
TOKENS = OWN * BLOCK
FIXED = (-1, 0, 1, 6, -6)
EITHER = ((2, 3), (-2, -3), (4, 9), (-4, -9), (8, 12), (-8, -12), (10, 15), (-10, -15))
LISTED = len(FIXED) + len(EITHER)
f32 = jnp.float32
bf16 = jnp.bfloat16
MESH = pl.DeviceIdType.MESH
BATCH = 4


def index_of(y, x, z):
    return lax.rem(y + NY, NY) * (NX * NZ) + lax.rem(x + NX, NX) * NZ + lax.rem(z, NZ)


def dot(a, b, ca, cb):
    return lax.dot_general(a, b, (((ca,), (cb,)), ((), ())), preferred_element_type=f32)


def kernel(
    key_blocks, tau_ref, queries, keys, values, grads,
    attended, query_grad, key_grad, value_grad, tau_out,
    kw, vw, q_all, g_all, s_all, high_all, e_scr, dk_acc, dv_acc, od,
    stage, arrived, z_stage, z_arrived, final, tau_acc, tau_x, tau_y, tau_z,
    here_sem, in_send, in_recv, od_send, od_recv, out_send, out_recv, tau_send, tau_recv,
):
    me = lax.axis_index("ctx")
    batch = lax.axis_index("batch")
    y, x, z = me // (NX * NZ), lax.rem(me // NZ, NX), lax.rem(me, NZ)

    def at(dy, dx, dz):
        return {"ctx": index_of(y + dy, x + dx, z + dz)}

    def far(dz, db):
        return {"ctx": index_of(y, x, z + dz), "batch": lax.rem(batch + db, BATCH)}

    def remote(src, dst, send, recv, device):
        return pltpu.make_async_remote_copy(
            src_ref=src, dst_ref=dst, send_sem=send, recv_sem=recv,
            device_id=device, device_id_type=MESH,
        )

    near_half = PLANE + z * HALF
    other_half = PLANE + (1 - z) * HALF

    def columns(array, n, place, width):
        return array.at[n, :, pl.ds(pl.multiple_of(place * width, width), width)]

    here_k, here_v, here_q, here_g = [
        [
            pltpu.make_async_copy(columns(array, n, x, width), place(0, n), here_sem.at[2 * i + n])
            for n in range(OWN)
        ]
        for i, (array, width, place) in enumerate(
            (
                (keys, HD, lambda d, n: kw.at[near_half + x * OWN + n]),
                (values, HD, lambda d, n: vw.at[near_half + x * OWN + n]),
                (queries, WIDE, lambda d, n: q_all.at[d * OWN + n]),
                (grads, WIDE, lambda d, n: g_all.at[d * OWN + n]),
            )
        )
    ]
    here = here_k + here_v + here_q + here_g
    for copy in here:
        copy.start()

    partners = [at(0, d, 0) for d in (1, 2, 3)] + [at(d, 0, 0) for d in (1, 2, 3)]
    partners += [far(dz, db) for dz in range(NZ) for db in range(BATCH) if dz or db]
    barrier = pltpu.get_barrier_semaphore()
    for device in partners:
        pl.semaphore_signal(barrier, inc=1, device_id=device, device_id_type=MESH)
    pl.semaphore_wait(barrier, len(partners))

    def along_x(array, width, place, first):
        out = []
        for d in (1, 2, 3):
            to = lax.rem(x + d, NX)
            for n in range(OWN):
                i = first + (d - 1) * OWN + n
                out.append(
                    remote(columns(array, n, to, width), place(d, n), in_send.at[i], in_recv.at[i], at(0, d, 0))
                )
        return out

    k_x = along_x(keys, HD, lambda d, n: kw.at[near_half + x * OWN + n], 0)
    v_x = along_x(values, HD, lambda d, n: vw.at[near_half + x * OWN + n], 6)
    q_x = along_x(queries, WIDE, lambda d, n: q_all.at[d * OWN + n], 12)
    g_x = along_x(grads, WIDE, lambda d, n: g_all.at[d * OWN + n], 18)

    def plane_sends(window, n):
        own = [
            remote(window.at[pl.ds(near_half, HALF)], window.at[pl.ds(near_half, HALF)], in_send.at[n], in_recv.at[n], at(0, 0, 1)),
            remote(window.at[pl.ds(near_half, HALF)], window.at[pl.ds(near_half - PLANE, HALF)], in_send.at[n + 1], in_recv.at[n + 1], at(1, 0, 0)),
            remote(window.at[pl.ds(near_half, HALF)], window.at[pl.ds(near_half + PLANE, HALF)], in_send.at[n + 2], in_recv.at[n + 2], at(3, 0, 0)),
        ]
        other = [
            remote(window.at[pl.ds(other_half, HALF)], window.at[pl.ds(other_half - PLANE, HALF)], in_send.at[n + 3], in_recv.at[n + 3], at(1, 0, 0)),
            remote(window.at[pl.ds(other_half, HALF)], window.at[pl.ds(other_half + PLANE, HALF)], in_send.at[n + 4], in_recv.at[n + 4], at(3, 0, 0)),
        ]
        return own, other

    k_own, k_other = plane_sends(kw, 24)
    v_own, v_other = plane_sends(vw, 29)

    def start(copies):
        for copy in copies:
            copy.start()

    def received(copies):
        for copy in copies:
            copy.wait_recv()

    start(k_x)
    start(v_x)
    for copy in here_k:
        copy.wait()
    received(k_x)
    start(k_own)
    for copy in here_v:
        copy.wait()
    received(v_x)
    start(q_x)
    received(k_own[:1])
    start(k_other)
    start(v_own)
    start(g_x)

    dk_acc[...] = jnp.zeros_like(dk_acc)
    dv_acc[...] = jnp.zeros_like(dv_acc)
    tau_acc[...] = jnp.zeros_like(tau_acc)
    scale = jnp.concatenate(
        [jnp.full((1, BLOCK), tau_ref[x * PER + h] / math.sqrt(HD), f32) for h in range(PER)], 1
    )

    def row_place(r):
        return lax.rem(x - r // OWN + NX, NX) * (NZ * OWN) + z * OWN + lax.rem(r, OWN)

    def slot_of(linear):
        rest = lax.rem(linear, PLANE)
        return (linear // PLANE) * PLANE + lax.rem(rest // OWN, NZ) * HALF + (rest // (NZ * OWN)) * OWN + lax.rem(rest, OWN)

    def is_two(r):
        a = y * PLANE + row_place(r)
        sought = lax.rem(a + 2, BLOCKS)
        hit = 0
        for k in range(LISTED):
            hit = jnp.where(key_blocks[x, a, k] == sought, 1, hit)
        return hit

    def slots(r):
        linear = PLANE + row_place(r)
        return (
            [slot_of(linear + o) for o in FIXED],
            [(slot_of(linear + two), slot_of(linear + three)) for two, three in EITHER],
        )

    def listed_slots(fixed, either, two):
        return fixed + [jnp.where(two == 1, p, q) for p, q in either]

    def heads_of(array, r):
        return jnp.concatenate([array[r, :, h * HD : (h + 1) * HD] for h in range(PER)], 0)

    def scores(r, _):
        q = heads_of(q_all, r)
        picks = listed_slots(*slots(r), is_two(r))
        high = None
        for k, slot in enumerate(picks):
            s = dot(kw[slot], q, 1, 1)
            s_all[r, k] = s
            top = s.reshape(16, 8, WIDE).max(0)
            high = top if high is None else jnp.maximum(high, top)
        high_all[r] = high
        return 0

    for copy in here_q:
        copy.wait()
    received(q_x)
    received(k_own[1:])
    received(k_other)
    lax.fori_loop(0, ROWS // 2, scores, 0)
    received(v_own[:1])
    start(v_other)
    lax.fori_loop(ROWS // 2, ROWS, scores, 0)
    for copy in here_g:
        copy.wait()
    received(g_x)
    received(v_own[1:])
    received(v_other)

    def back(r, which, out, local):
        d, half = r // OWN, lax.rem(r, OWN)
        dst = columns(out, half, x, WIDE)
        n = which * ROWS + r
        if local:
            return pltpu.make_async_copy(od.at[r, which], dst, od_recv.at[n])
        return remote(od.at[r, which], dst, od_send.at[n], od_recv.at[n], at(0, NX - d, 0))

    def send_back(r, which, out):
        @pl.when(r < OWN)
        def _():
            back(r, which, out, True).start()

        @pl.when(r >= OWN)
        def _():
            back(r, which, out, False).start()

    def row(step, _):
        r = lax.rem(step + OWN, ROWS)
        q = heads_of(q_all, r)
        g = heads_of(g_all, r)
        fixed, either = slots(r)
        two = is_two(r)
        picks = listed_slots(fixed, either, two)
        weight = two.astype(f32)

        def add(acc, k, part):
            if k < len(FIXED):
                acc[fixed[k]] += part
            else:
                p, q = either[k - len(FIXED)]
                acc[p] += part * weight
                acc[q] += part * (1.0 - weight)

        high = high_all[r].max(0, keepdims=True)
        total = jnp.zeros((8, WIDE), f32)
        for k in range(LISTED):
            e = jnp.exp((s_all[r, k] - high) * scale)
            e_scr[k] = e
            total = total + e.reshape(16, 8, WIDE).sum(0)
        inverse = 1.0 / total.sum(0, keepdims=True)
        o = None
        for k in range(LISTED):
            p = (e_scr[k] * inverse).astype(bf16)
            add(dv_acc, k, dot(p, g, 1, 0))
            part = dot(p, vw[picks[k]], 0, 0)
            o = part if o is None else o + part
        for h in range(PER):
            od[r, 0, :, h * HD : (h + 1) * HD] = o[h * BLOCK : (h + 1) * BLOCK].astype(bf16)
        send_back(r, 0, attended)
        row_dot = (g.astype(f32) * o).sum(-1, keepdims=True)
        row_dot = jnp.broadcast_to(row_dot, (WIDE, HD)).T[0:1]
        tau = jnp.zeros((8, WIDE), f32)
        dq = None
        factor = inverse * scale
        for k in range(LISTED):
            t = e_scr[k] * (dot(vw[picks[k]], g, 1, 1) - row_dot)
            tau = tau + (t * s_all[r, k]).reshape(16, 8, WIDE).sum(0)
            ds = (t * factor).astype(bf16)
            add(dk_acc, k, dot(ds, q, 1, 0))
            part = dot(ds, kw[picks[k]], 0, 0)
            dq = part if dq is None else dq + part
        for h in range(PER):
            od[r, 1, :, h * HD : (h + 1) * HD] = dq[h * BLOCK : (h + 1) * BLOCK].astype(bf16)
        send_back(r, 1, query_grad)
        tau_acc[...] += tau * inverse
        return 0

    lax.fori_loop(0, ROWS, row, 0)

    accs = (dv_acc, dk_acc)
    y_out = []
    for kv in range(2):
        for half in range(2):
            for side in range(2):
                n = kv * 4 + half * 2 + side
                begin = side * 2 * PLANE + (1 - z if half == 0 else z) * HALF
                stage[n] = accs[kv][pl.ds(begin, HALF)].astype(bf16)
                copy = remote(stage.at[n], arrived.at[n], out_send.at[n], out_recv.at[n], at(3 if side == 0 else 1, 0, 0))
                copy.start()
                y_out.append(copy)

    tau_waits = []
    parts = jnp.concatenate([tau_acc[:, h * BLOCK : (h + 1) * BLOCK].sum(0, keepdims=True) for h in range(PER)], 0)
    tau_x[x] = jnp.concatenate([parts, jnp.zeros_like(parts)], 0)
    tau_first = [remote(tau_x.at[x], tau_x.at[x], tau_send.at[d - 1], tau_recv.at[d - 1], at(0, d, 0)) for d in (1, 2, 3)]
    start(tau_first)
    received(tau_first)
    tau_y[y] = tau_x[...]
    tau_second = [remote(tau_y.at[y], tau_y.at[y], tau_send.at[d + 2], tau_recv.at[d + 2], at(d, 0, 0)) for d in (1, 2, 3)]
    start(tau_second)

    z_out = []
    for kv in range(2):
        received(y_out[kv * 4 : kv * 4 + 2])
        summed = accs[kv][pl.ds(other_half, HALF)] + arrived[kv * 4].astype(f32) + arrived[kv * 4 + 1].astype(f32)
        z_stage[kv] = summed.astype(bf16)
        copy = remote(z_stage.at[kv], z_arrived.at[kv], out_send.at[8 + kv], out_recv.at[8 + kv], at(0, 0, 1))
        copy.start()
        z_out.append(copy)

    received(tau_second)
    spot = z * BATCH + batch
    tau_z[spot] = tau_y[0] + tau_y[1] + tau_y[2] + tau_y[3]
    tau_third = []
    for dz in range(NZ):
        for db in range(BATCH):
            if dz or db:
                n = 6 + len(tau_third)
                tau_third.append(remote(tau_z.at[spot], tau_z.at[spot], tau_send.at[n], tau_recv.at[n], far(dz, db)))
    start(tau_third)

    x_out = []
    x_local = []
    for kv, out in enumerate((value_grad, key_grad)):
        received(y_out[kv * 4 + 2 : kv * 4 + 4])
        received(z_out[kv : kv + 1])
        summed = accs[kv][pl.ds(near_half, HALF)] + arrived[kv * 4 + 2].astype(f32) + arrived[kv * 4 + 3].astype(f32)
        final[kv] = (summed + z_arrived[kv].astype(f32)).astype(bf16)
        for d in range(NX):
            from_x = lax.rem(x - d + NX, NX)
            for m in range(OWN):
                src = final.at[kv, from_x * OWN + m]
                dst = columns(out, m, x, HD)
                n = 10 + (kv * NX + d) * OWN + m
                if d == 0:
                    copy = pltpu.make_async_copy(src, dst, out_recv.at[n])
                    x_local.append(copy)
                else:
                    copy = remote(src, dst, out_send.at[n], out_recv.at[n], at(0, NX - d, 0))
                    x_out.append(copy)
                copy.start()

    received(tau_third)
    whole = tau_z[0]
    for n in range(1, NZ * BATCH):
        whole = whole + tau_z[n]
    norm = math.sqrt(HD) * math.sqrt(BATCH * NY * NX * NZ * TOKENS)
    for n in range(NX):
        for h in range(PER):
            tau_out[n * PER + h] = jnp.sum(whole[n, h : h + 1, :]) / norm

    received(x_out)
    for copy in x_local:
        copy.wait()
    for which, out in enumerate((attended, query_grad)):
        for r in range(ROWS):
            back(r, which, out, r < OWN).wait()
    for copy in k_x + v_x + q_x + g_x + k_own + k_other + v_own + v_other:
        copy.wait_send()
    for copy in y_out + z_out + x_out + tau_first + tau_second + tau_third:
        copy.wait_send()


def body(queries, keys, values, tau, out_grad, key_blocks):
    anywhere = pl.BlockSpec(memory_space=pl.ANY)
    scalars = pl.BlockSpec(memory_space=pltpu.SMEM)
    shape = lambda a: (OWN, BLOCK, a.shape[2])
    half = (HALF, BLOCK, HD)
    blocked = [a.reshape(shape(a)) for a in (queries, keys, values, out_grad)]
    outs = pl.pallas_call(
        kernel,
        name="attention",
        out_shape=(
            jax.ShapeDtypeStruct(shape(queries), bf16),
            jax.ShapeDtypeStruct(shape(queries), bf16),
            jax.ShapeDtypeStruct(shape(keys), bf16),
            jax.ShapeDtypeStruct(shape(keys), bf16),
            jax.ShapeDtypeStruct((HEADS,), f32),
        ),
        in_specs=[scalars, scalars] + [anywhere] * 4,
        out_specs=(anywhere,) * 4 + (scalars,),
        scratch_shapes=[
            pltpu.VMEM((WINDOW, BLOCK, HD), bf16),
            pltpu.VMEM((WINDOW, BLOCK, HD), bf16),
            pltpu.VMEM((ROWS, BLOCK, WIDE), bf16),
            pltpu.VMEM((ROWS, BLOCK, WIDE), bf16),
            pltpu.VMEM((ROWS, LISTED, BLOCK, WIDE), f32),
            pltpu.VMEM((ROWS, 8, WIDE), f32),
            pltpu.VMEM((LISTED, BLOCK, WIDE), f32),
            pltpu.VMEM((WINDOW, BLOCK, HD), f32),
            pltpu.VMEM((WINDOW, BLOCK, HD), f32),
            pltpu.VMEM((ROWS, 2, BLOCK, WIDE), bf16),
            pltpu.VMEM((8,) + half, bf16),
            pltpu.VMEM((8,) + half, bf16),
            pltpu.VMEM((2,) + half, bf16),
            pltpu.VMEM((2,) + half, bf16),
            pltpu.VMEM((2,) + half, bf16),
            pltpu.VMEM((8, WIDE), f32),
            pltpu.VMEM((NX, 8, BLOCK), f32),
            pltpu.VMEM((NY, NX, 8, BLOCK), f32),
            pltpu.VMEM((NZ * BATCH, NX, 8, BLOCK), f32),
            pltpu.SemaphoreType.DMA((8,)),
            pltpu.SemaphoreType.DMA((34,)),
            pltpu.SemaphoreType.DMA((34,)),
            pltpu.SemaphoreType.DMA((2 * ROWS,)),
            pltpu.SemaphoreType.DMA((2 * ROWS,)),
            pltpu.SemaphoreType.DMA((26,)),
            pltpu.SemaphoreType.DMA((26,)),
            pltpu.SemaphoreType.DMA((13,)),
            pltpu.SemaphoreType.DMA((13,)),
        ],
        compiler_params=pltpu.CompilerParams(
            collective_id=0, has_side_effects=True, vmem_limit_bytes=62 << 20
        ),
    )(key_blocks, tau, *blocked)
    return tuple(o.reshape(a.shape) for o, a in zip(outs[:4], (queries, queries, keys, keys))) + (outs[4],)


def solution(mesh):
    sharded = P("batch", "ctx", None)
    return jax.shard_map(
        body,
        mesh=mesh,
        in_specs=(sharded, sharded, sharded, P(), sharded, P()),
        out_specs=(sharded, sharded, sharded, sharded, P()),
        check_vma=False,
    )
```

```python
import math

import jax
import jax.numpy as jnp
from jax import lax
from jax.experimental import pallas as pl
from jax.experimental.pallas import tpu as pltpu
from jax.sharding import PartitionSpec as P

HEADS = 16
GROUPS = 4
PER = HEADS // GROUPS
HD = 128
BLOCK = 128
BLOCKS = 64
WIDE = PER * HD
NY, NX, NZ = 4, 4, 2
OWN = 2
ROWS = NX * OWN
HALF = NX * OWN
PLANE = NZ * HALF
WINDOW = 3 * PLANE
TOKENS = OWN * BLOCK
FIXED = (-1, 0, 1, 6, -6)
EITHER = ((2, 3), (-2, -3), (4, 9), (-4, -9), (8, 12), (-8, -12), (10, 15), (-10, -15))
LISTED = len(FIXED) + len(EITHER)
f32 = jnp.float32
bf16 = jnp.bfloat16
LOG2E = math.log2(math.e)
MESH = pl.DeviceIdType.MESH
BATCH = 4


def index_of(y, x, z):
    return lax.rem(y + NY, NY) * (NX * NZ) + lax.rem(x + NX, NX) * NZ + lax.rem(z, NZ)


def dot(a, b, ca, cb):
    return lax.dot_general(a, b, (((ca,), (cb,)), ((), ())), preferred_element_type=f32)


def kernel(
    key_blocks, tau_ref, queries, keys, values, grads,
    attended, query_grad, key_grad, value_grad, tau_out,
    kw, vw, q_all, g_all, s_all, ds_all, shift_all, dot_all, dk_acc, dv_acc, od,
    stage, arrived, z_stage, z_arrived, final, tau_acc, tau_x, tau_y, tau_z,
    here_sem, in_send, in_recv, od_send, od_recv, out_send, out_recv, tau_send, tau_recv,
):
    me = lax.axis_index("ctx")
    batch = lax.axis_index("batch")
    y, x, z = me // (NX * NZ), lax.rem(me // NZ, NX), lax.rem(me, NZ)

    def at(dy, dx, dz):
        return {"ctx": index_of(y + dy, x + dx, z + dz)}

    def far(dz, db):
        return {"ctx": index_of(y, x, z + dz), "batch": lax.rem(batch + db, BATCH)}

    def remote(src, dst, send, recv, device):
        return pltpu.make_async_remote_copy(
            src_ref=src, dst_ref=dst, send_sem=send, recv_sem=recv,
            device_id=device, device_id_type=MESH,
        )

    near_half = PLANE + z * HALF
    other_half = PLANE + (1 - z) * HALF

    def columns(array, n, place, width):
        return array.at[n, :, pl.ds(pl.multiple_of(place * width, width), width)]

    here_k, here_v, here_q, here_g = [
        [
            pltpu.make_async_copy(columns(array, n, x, width), place(0, n), here_sem.at[2 * i + n])
            for n in range(OWN)
        ]
        for i, (array, width, place) in enumerate(
            (
                (keys, HD, lambda d, n: kw.at[near_half + x * OWN + n]),
                (values, HD, lambda d, n: vw.at[near_half + x * OWN + n]),
                (queries, WIDE, lambda d, n: q_all.at[d * OWN + n]),
                (grads, WIDE, lambda d, n: g_all.at[d * OWN + n]),
            )
        )
    ]
    here = here_k + here_v + here_q + here_g
    for copy in here:
        copy.start()

    partners = [at(0, d, 0) for d in (1, 2, 3)] + [at(d, 0, 0) for d in (1, 2, 3)]
    partners += [far(dz, db) for dz in range(NZ) for db in range(BATCH) if dz or db]
    barrier = pltpu.get_barrier_semaphore()
    for device in partners:
        pl.semaphore_signal(barrier, inc=1, device_id=device, device_id_type=MESH)
    pl.semaphore_wait(barrier, len(partners))

    def along_x(array, width, place, first):
        out = []
        for d in (1, 2, 3):
            to = lax.rem(x + d, NX)
            for n in range(OWN):
                i = first + (d - 1) * OWN + n
                out.append(
                    remote(columns(array, n, to, width), place(d, n), in_send.at[i], in_recv.at[i], at(0, d, 0))
                )
        return out

    k_x = along_x(keys, HD, lambda d, n: kw.at[near_half + x * OWN + n], 0)
    v_x = along_x(values, HD, lambda d, n: vw.at[near_half + x * OWN + n], 6)
    q_x = along_x(queries, WIDE, lambda d, n: q_all.at[d * OWN + n], 12)
    g_x = along_x(grads, WIDE, lambda d, n: g_all.at[d * OWN + n], 18)

    def plane_sends(window, n):
        own = [
            remote(window.at[pl.ds(near_half, HALF)], window.at[pl.ds(near_half, HALF)], in_send.at[n], in_recv.at[n], at(0, 0, 1)),
            remote(window.at[pl.ds(near_half, HALF)], window.at[pl.ds(near_half - PLANE, HALF)], in_send.at[n + 1], in_recv.at[n + 1], at(1, 0, 0)),
            remote(window.at[pl.ds(near_half, HALF)], window.at[pl.ds(near_half + PLANE, HALF)], in_send.at[n + 2], in_recv.at[n + 2], at(3, 0, 0)),
        ]
        other = [
            remote(window.at[pl.ds(other_half, HALF)], window.at[pl.ds(other_half - PLANE, HALF)], in_send.at[n + 3], in_recv.at[n + 3], at(1, 0, 0)),
            remote(window.at[pl.ds(other_half, HALF)], window.at[pl.ds(other_half + PLANE, HALF)], in_send.at[n + 4], in_recv.at[n + 4], at(3, 0, 0)),
        ]
        return own, other

    k_own, k_other = plane_sends(kw, 24)
    v_own, v_other = plane_sends(vw, 29)

    def start(copies):
        for copy in copies:
            copy.start()

    def received(copies):
        for copy in copies:
            copy.wait_recv()

    def wait(copies):
        for copy in copies:
            copy.wait()

    q_even, q_odd = q_x[0::OWN], q_x[1::OWN]
    start(k_x)
    dk_acc[...] = jnp.zeros_like(dk_acc)
    dv_acc[...] = jnp.zeros_like(dv_acc)
    scale = jnp.concatenate(
        [jnp.full((1, BLOCK), tau_ref[x * PER + h] / math.sqrt(HD), f32) for h in range(PER)], 1
    )
    scale_two = scale * LOG2E
    wait(here_k)
    received(k_x)
    start(k_own)
    start(q_even)
    start(v_x)
    received(k_own[:1])
    start(k_other)
    wait(here_v)
    received(q_even)
    received(v_x)
    start(v_own[:1])
    start(q_odd)
    wait(here_q)
    received(k_own[1:])
    received(k_other)
    start(v_own[1:])

    def row_place(r):
        return lax.rem(x - r // OWN + NX, NX) * (NZ * OWN) + z * OWN + lax.rem(r, OWN)

    def slot_of(linear):
        rest = lax.rem(linear, PLANE)
        return (linear // PLANE) * PLANE + lax.rem(rest // OWN, NZ) * HALF + (rest // (NZ * OWN)) * OWN + lax.rem(rest, OWN)

    def is_two(r):
        a = y * PLANE + row_place(r)
        sought = lax.rem(a + 2, BLOCKS)
        hit = 0
        for k in range(LISTED):
            hit = jnp.where(key_blocks[k, x, a] == sought, 1, hit)
        return hit

    def slots(r):
        linear = PLANE + row_place(r)
        fixed = [slot_of(linear + o) for o in FIXED]
        either = [(slot_of(linear + two), slot_of(linear + three)) for two, three in EITHER]
        two = is_two(r)
        picks = fixed + [jnp.where(two == 1, p, q) for p, q in either]
        weight = two.astype(f32)

        def add(acc, k, part):
            if k < len(FIXED):
                acc[fixed[k]] += part
            else:
                p, q = either[k - len(FIXED)]
                acc[p] += part * weight
                acc[q] += part * (1.0 - weight)

        return picks, add

    def heads_of(array, r):
        return jnp.concatenate([array[r, :, h * HD : (h + 1) * HD] for h in range(PER)], 0)

    def folded(array):
        return array.reshape(BLOCK // 8, 8, WIDE)

    def scores(r):
        q = heads_of(q_all, r)
        picks, _ = slots(r)
        high = None
        for k in range(LISTED):
            s = dot(kw[picks[k]], q, 1, 1)
            s_all[r, k] = s
            top = folded(s).max(0)
            high = top if high is None else jnp.maximum(high, top)
        high = high.max(0, keepdims=True)
        total = jnp.zeros((8, WIDE), f32)
        for k in range(LISTED):
            total = total + folded(jnp.exp2((s_all[r, k] - high) * scale_two)).sum(0)
        log_total = jnp.log(total.sum(0, keepdims=True)) * LOG2E
        for k in range(LISTED):
            s_all[r, k] = (s_all[r, k] - high) * scale_two - log_total
        shift_all[r] = jnp.broadcast_to(high + log_total / scale_two, (8, WIDE))

    def even_scores(i, _):
        @pl.when(i == 1)
        def _():
            received(q_odd)
            start(g_x)

        @pl.when(i == 2)
        def _():
            received(v_own[:1])
            start(v_other)

        scores(i * OWN)
        return 0

    def odd_scores(i, _):
        scores(i * OWN + 1)
        return 0

    lax.fori_loop(0, NX, even_scores, 0)
    lax.fori_loop(0, NX, odd_scores, 0)
    wait(here_g)
    received(g_x)
    received(v_own[1:])
    received(v_other)

    def back(r, which, out, local):
        d, half = r // OWN, lax.rem(r, OWN)
        dst = columns(out, half, x, WIDE)
        n = which * ROWS + r
        if local:
            return pltpu.make_async_copy(od.at[r, which], dst, od_recv.at[n])
        return remote(od.at[r, which], dst, od_send.at[n], od_recv.at[n], at(0, NX - d, 0))

    def send_back(r, which, out, result):
        for h in range(PER):
            od[r, which, :, h * HD : (h + 1) * HD] = result[h * BLOCK : (h + 1) * BLOCK].astype(bf16)

        @pl.when(r < OWN)
        def _():
            back(r, which, out, True).start()

        @pl.when(r >= OWN)
        def _():
            back(r, which, out, False).start()

    def outputs(step, _):
        r = lax.rem(step + OWN, ROWS)
        g = heads_of(g_all, r)
        picks, add = slots(r)
        o = None
        for k in range(LISTED):
            p = jnp.exp2(s_all[r, k]).astype(bf16)
            add(dv_acc, k, dot(p, g, 1, 0))
            part = dot(p, vw[picks[k]], 0, 0)
            o = part if o is None else o + part
        send_back(r, 0, attended, o)
        row_dot = (g.astype(f32) * o).sum(-1, keepdims=True)
        dot_all[r] = jnp.broadcast_to(row_dot, (WIDE, HD)).T[0:8]
        return 0

    lax.fori_loop(0, ROWS, outputs, 0)

    accs = (dv_acc, dk_acc)
    outs = (value_grad, key_grad)

    def y_copy(kv, half, side):
        n = kv * 4 + half * 2 + side
        return remote(stage.at[n], arrived.at[n], out_send.at[n], out_recv.at[n], at(3 if side == 0 else 1, 0, 0))

    def y_pair(kv, half):
        return [y_copy(kv, half, side) for side in range(2)]

    def z_copy(kv):
        return remote(z_stage.at[kv], z_arrived.at[kv], out_send.at[8 + kv], out_recv.at[8 + kv], at(0, 0, 1))

    def x_copies(kv, local):
        copies = []
        for d in range(NX):
            from_x = lax.rem(x - d + NX, NX)
            for m in range(OWN):
                src = final.at[kv, from_x * OWN + m]
                dst = columns(outs[kv], m, x, HD)
                n = 10 + (kv * NX + d) * OWN + m
                if local and d == 0:
                    copies.append(pltpu.make_async_copy(src, dst, out_recv.at[n]))
                if not local and d > 0:
                    copies.append(remote(src, dst, out_send.at[n], out_recv.at[n], at(0, NX - d, 0)))
        return copies

    def to_y(kv):
        for half in range(2):
            for side in range(2):
                begin = side * 2 * PLANE + (1 - z if half == 0 else z) * HALF
                stage[kv * 4 + half * 2 + side] = accs[kv][pl.ds(begin, HALF)].astype(bf16)
                y_copy(kv, half, side).start()

    def to_z(kv):
        received(y_pair(kv, 0))
        summed = accs[kv][pl.ds(other_half, HALF)] + arrived[kv * 4].astype(f32) + arrived[kv * 4 + 1].astype(f32)
        z_stage[kv] = summed.astype(bf16)
        z_copy(kv).start()

    def to_x(kv):
        received(y_pair(kv, 1))
        summed = accs[kv][pl.ds(near_half, HALF)] + arrived[kv * 4 + 2].astype(f32) + arrived[kv * 4 + 3].astype(f32)
        z_copy(kv).wait_recv()
        final[kv] = (summed + z_arrived[kv].astype(f32)).astype(bf16)
        start(x_copies(kv, False))
        start(x_copies(kv, True))

    to_y(0)
    tau_acc[...] = jnp.zeros_like(tau_acc)

    def score_grads(step, _):
        @pl.when(step == 4)
        def _():
            to_z(0)

        @pl.when(step == 7)
        def _():
            to_x(0)

        r = step
        q = heads_of(q_all, r)
        g = heads_of(g_all, r)
        picks, add = slots(r)
        row_dot = dot_all[r][0:1]
        first = jnp.zeros((8, WIDE), f32)
        second = jnp.zeros((8, WIDE), f32)
        for k in range(LISTED):
            s = s_all[r, k]
            t = jnp.exp2(s) * (dot(vw[picks[k]], g, 1, 1) - row_dot)
            first = first + folded(t * s).sum(0)
            second = second + folded(t).sum(0)
            ds = (t * scale).astype(bf16)
            ds_all[r, k] = ds
            add(dk_acc, k, dot(ds, q, 1, 0))
        tau_acc[...] += first / scale_two + second * shift_all[r]
        return 0

    lax.fori_loop(0, ROWS, score_grads, 0)
    to_y(1)

    parts = jnp.concatenate([tau_acc[:, h * BLOCK : (h + 1) * BLOCK].sum(0, keepdims=True) for h in range(PER)], 0)
    tau_x[x] = jnp.concatenate([parts, jnp.zeros_like(parts)], 0)
    tau_first = [remote(tau_x.at[x], tau_x.at[x], tau_send.at[d - 1], tau_recv.at[d - 1], at(0, d, 0)) for d in (1, 2, 3)]
    start(tau_first)

    def query_grads(step, _):
        r = lax.rem(step + OWN, ROWS)
        picks, _ = slots(r)
        dq = None
        for k in range(LISTED):
            part = dot(ds_all[r, k], kw[picks[k]], 0, 0)
            dq = part if dq is None else dq + part
        send_back(r, 1, query_grad, dq)
        return 0

    lax.fori_loop(0, ROWS, query_grads, 0)
    to_z(1)
    received(tau_first)
    tau_y[y] = tau_x[...]
    tau_second = [remote(tau_y.at[y], tau_y.at[y], tau_send.at[d + 2], tau_recv.at[d + 2], at(d, 0, 0)) for d in (1, 2, 3)]
    start(tau_second)
    received(tau_second)
    spot = z * BATCH + batch
    tau_z[spot] = tau_y[0] + tau_y[1] + tau_y[2] + tau_y[3]
    tau_third = []
    for dz in range(NZ):
        for db in range(BATCH):
            if dz or db:
                n = 6 + len(tau_third)
                tau_third.append(remote(tau_z.at[spot], tau_z.at[spot], tau_send.at[n], tau_recv.at[n], far(dz, db)))
    start(tau_third)
    to_x(1)
    received(tau_third)
    whole = tau_z[0]
    for n in range(1, NZ * BATCH):
        whole = whole + tau_z[n]
    norm = math.sqrt(HD) * math.sqrt(BATCH * NY * NX * NZ * TOKENS)
    for n in range(NX):
        for h in range(PER):
            tau_out[n * PER + h] = jnp.sum(whole[n, h : h + 1, :]) / norm

    for which, out in enumerate((attended, query_grad)):
        for r in range(ROWS):
            back(r, which, out, r < OWN).wait()
    for kv in range(2):
        received(x_copies(kv, False))
        wait(x_copies(kv, True))
    sent = k_x + v_x + q_x + g_x + k_own + k_other + v_own + v_other + tau_first + tau_second + tau_third
    for kv in range(2):
        sent += y_pair(kv, 0) + y_pair(kv, 1) + [z_copy(kv)] + x_copies(kv, False)
    for copy in sent:
        copy.wait_send()


def copy_out(*refs):
    n = len(refs) // 2
    sems = refs[-1]
    copies = [pltpu.make_async_copy(refs[i], refs[n + i], sems.at[i]) for i in range(n)]
    for copy in copies:
        copy.start()
    for copy in copies:
        copy.wait()


def body(queries, keys, values, tau, out_grad, key_blocks):
    anywhere = pl.BlockSpec(memory_space=pl.ANY)
    scalars = pl.BlockSpec(memory_space=pltpu.SMEM)
    shape = lambda a: (OWN, BLOCK, a.shape[2])
    half = (HALF, BLOCK, HD)
    blocked = [a.reshape(shape(a)) for a in (queries, keys, values, out_grad)]
    outs = pl.pallas_call(
        kernel,
        name="attention",
        out_shape=(
            jax.ShapeDtypeStruct(shape(queries), bf16),
            jax.ShapeDtypeStruct(shape(queries), bf16),
            jax.ShapeDtypeStruct(shape(keys), bf16),
            jax.ShapeDtypeStruct(shape(keys), bf16),
            jax.ShapeDtypeStruct((HEADS,), f32),
        ),
        in_specs=[scalars, scalars] + [anywhere] * 4,
        out_specs=(anywhere,) * 4 + (scalars,),
        scratch_shapes=[
            pltpu.VMEM((WINDOW, BLOCK, HD), bf16),
            pltpu.VMEM((WINDOW, BLOCK, HD), bf16),
            pltpu.VMEM((ROWS, BLOCK, WIDE), bf16),
            pltpu.VMEM((ROWS, BLOCK, WIDE), bf16),
            pltpu.VMEM((ROWS, LISTED, BLOCK, WIDE), f32),
            pltpu.VMEM((ROWS, LISTED, BLOCK, WIDE), bf16),
            pltpu.VMEM((ROWS, 8, WIDE), f32),
            pltpu.VMEM((ROWS, 8, WIDE), f32),
            pltpu.VMEM((WINDOW, BLOCK, HD), f32),
            pltpu.VMEM((WINDOW, BLOCK, HD), f32),
            pltpu.VMEM((ROWS, 2, BLOCK, WIDE), bf16),
            pltpu.VMEM((8,) + half, bf16),
            pltpu.VMEM((8,) + half, bf16),
            pltpu.VMEM((2,) + half, bf16),
            pltpu.VMEM((2,) + half, bf16),
            pltpu.VMEM((2,) + half, bf16),
            pltpu.VMEM((8, WIDE), f32),
            pltpu.VMEM((NX, 8, BLOCK), f32),
            pltpu.VMEM((NY, NX, 8, BLOCK), f32),
            pltpu.VMEM((NZ * BATCH, NX, 8, BLOCK), f32),
            pltpu.SemaphoreType.DMA((8,)),
            pltpu.SemaphoreType.DMA((34,)),
            pltpu.SemaphoreType.DMA((34,)),
            pltpu.SemaphoreType.DMA((2 * ROWS,)),
            pltpu.SemaphoreType.DMA((2 * ROWS,)),
            pltpu.SemaphoreType.DMA((26,)),
            pltpu.SemaphoreType.DMA((26,)),
            pltpu.SemaphoreType.DMA((13,)),
            pltpu.SemaphoreType.DMA((13,)),
        ],
        compiler_params=pltpu.CompilerParams(
            collective_id=0, has_side_effects=True, vmem_limit_bytes=62 << 20
        ),
    )(key_blocks.transpose(2, 0, 1), tau, *blocked)
    outs = pl.pallas_call(
        copy_out,
        name="copy_out",
        out_shape=tuple(jax.ShapeDtypeStruct(o.shape, o.dtype) for o in outs),
        in_specs=[anywhere] * len(outs),
        out_specs=(anywhere,) * len(outs),
        scratch_shapes=[pltpu.SemaphoreType.DMA((len(outs),))],
    )(*outs)
    return tuple(o.reshape(a.shape) for o, a in zip(outs[:4], (queries, queries, keys, keys))) + (outs[4],)


def solution(mesh):
    sharded = P("batch", "ctx", None)
    return jax.shard_map(
        body,
        mesh=mesh,
        in_specs=(sharded, sharded, sharded, P(), sharded, P()),
        out_specs=(sharded, sharded, sharded, sharded, P()),
        check_vma=False,
    )
```

```python
import math

import jax
import jax.numpy as jnp
from jax import lax
from jax.experimental import pallas as pl
from jax.experimental.pallas import tpu as pltpu
from jax.sharding import PartitionSpec as P

HEADS = 16
GROUPS = 4
PER = HEADS // GROUPS
HD = 128
BLOCK = 128
BLOCKS = 64
WIDE = PER * HD
NY, NX, NZ = 4, 4, 2
OWN = 2
ROWS = NX * OWN
HALF = NX * OWN
PLANE = NZ * HALF
WINDOW = 3 * PLANE
PARTS = 2
CHUNK = HALF // PARTS
TOKENS = OWN * BLOCK
FIXED = (-1, 0, 1, 6, -6)
EITHER = ((2, 3), (-2, -3), (4, 9), (-4, -9), (8, 12), (-8, -12), (10, 15), (-10, -15))
LISTED = len(FIXED) + len(EITHER)
f32 = jnp.float32
bf16 = jnp.bfloat16
LOG2E = math.log2(math.e)
MESH = pl.DeviceIdType.MESH
BATCH = 4


def index_of(y, x, z):
    return lax.rem(y + NY, NY) * (NX * NZ) + lax.rem(x + NX, NX) * NZ + lax.rem(z, NZ)


def dot(a, b, ca, cb):
    return lax.dot_general(a, b, (((ca,), (cb,)), ((), ())), preferred_element_type=f32)


def kernel(
    key_blocks, tau_ref, queries, keys, values, grads,
    attended, query_grad, key_grad, value_grad, tau_out,
    kw, vw, q_all, g_all, s_all, ds_all, shift_all, dot_all, dk_acc, dv_acc, od,
    stage, arrived, z_stage, z_arrived, final, tau_acc, tau_x, tau_y, tau_z,
    here_sem, in_send, in_recv, od_send, od_recv, y_send, y_recv, z_send, z_recv, x_send, x_recv, tau_send, tau_recv,
):
    me = lax.axis_index("ctx")
    batch = lax.axis_index("batch")
    y, x, z = me // (NX * NZ), lax.rem(me // NZ, NX), lax.rem(me, NZ)

    def at(dy, dx, dz):
        return {"ctx": index_of(y + dy, x + dx, z + dz)}

    def far(dz, db):
        return {"ctx": index_of(y, x, z + dz), "batch": lax.rem(batch + db, BATCH)}

    def remote(src, dst, send, recv, device):
        return pltpu.make_async_remote_copy(
            src_ref=src, dst_ref=dst, send_sem=send, recv_sem=recv,
            device_id=device, device_id_type=MESH,
        )

    near_half = PLANE + z * HALF
    other_half = PLANE + (1 - z) * HALF

    def columns(array, n, place, width):
        return array.at[n, :, pl.ds(pl.multiple_of(place * width, width), width)]

    here_k, here_v, here_q, here_g = [
        [
            pltpu.make_async_copy(columns(array, n, x, width), place(0, n), here_sem.at[2 * i + n])
            for n in range(OWN)
        ]
        for i, (array, width, place) in enumerate(
            (
                (keys, HD, lambda d, n: kw.at[near_half + x * OWN + n]),
                (values, HD, lambda d, n: vw.at[near_half + x * OWN + n]),
                (queries, WIDE, lambda d, n: q_all.at[d * OWN + n]),
                (grads, WIDE, lambda d, n: g_all.at[d * OWN + n]),
            )
        )
    ]
    here = here_k + here_v + here_q + here_g
    for copy in here:
        copy.start()

    partners = [at(0, d, 0) for d in (1, 2, 3)] + [at(d, 0, 0) for d in (1, 2, 3)]
    partners += [far(dz, db) for dz in range(NZ) for db in range(BATCH) if dz or db]
    barrier = pltpu.get_barrier_semaphore()
    for device in partners:
        pl.semaphore_signal(barrier, inc=1, device_id=device, device_id_type=MESH)
    pl.semaphore_wait(barrier, len(partners))

    def along_x(array, width, place, first):
        out = []
        for d in (1, 2, 3):
            to = lax.rem(x + d, NX)
            for n in range(OWN):
                i = first + (d - 1) * OWN + n
                out.append(
                    remote(columns(array, n, to, width), place(d, n), in_send.at[i], in_recv.at[i], at(0, d, 0))
                )
        return out

    k_x = along_x(keys, HD, lambda d, n: kw.at[near_half + x * OWN + n], 0)
    v_x = along_x(values, HD, lambda d, n: vw.at[near_half + x * OWN + n], 6)
    q_x = along_x(queries, WIDE, lambda d, n: q_all.at[d * OWN + n], 12)
    g_x = along_x(grads, WIDE, lambda d, n: g_all.at[d * OWN + n], 18)

    def plane_sends(window, n):
        own = [
            remote(window.at[pl.ds(near_half, HALF)], window.at[pl.ds(near_half, HALF)], in_send.at[n], in_recv.at[n], at(0, 0, 1)),
            remote(window.at[pl.ds(near_half, HALF)], window.at[pl.ds(near_half - PLANE, HALF)], in_send.at[n + 1], in_recv.at[n + 1], at(1, 0, 0)),
            remote(window.at[pl.ds(near_half, HALF)], window.at[pl.ds(near_half + PLANE, HALF)], in_send.at[n + 2], in_recv.at[n + 2], at(3, 0, 0)),
        ]
        other = [
            remote(window.at[pl.ds(other_half, HALF)], window.at[pl.ds(other_half - PLANE, HALF)], in_send.at[n + 3], in_recv.at[n + 3], at(1, 0, 0)),
            remote(window.at[pl.ds(other_half, HALF)], window.at[pl.ds(other_half + PLANE, HALF)], in_send.at[n + 4], in_recv.at[n + 4], at(3, 0, 0)),
        ]
        return own, other

    k_own, k_other = plane_sends(kw, 24)
    v_own, v_other = plane_sends(vw, 29)

    def start(copies):
        for copy in copies:
            copy.start()

    def received(copies):
        for copy in copies:
            copy.wait_recv()

    def wait(copies):
        for copy in copies:
            copy.wait()

    q_even, q_odd = q_x[0::OWN], q_x[1::OWN]
    start(k_x)
    dk_acc[...] = jnp.zeros_like(dk_acc)
    dv_acc[...] = jnp.zeros_like(dv_acc)
    scale = jnp.concatenate(
        [jnp.full((1, BLOCK), tau_ref[x * PER + h] / math.sqrt(HD), f32) for h in range(PER)], 1
    )
    scale_two = scale * LOG2E
    wait(here_k)
    received(k_x)
    start(k_own)
    start(v_x)
    start(q_even)
    wait(here_v)
    received(v_x)
    start(v_own)
    start(q_odd)
    start(g_x)
    received(k_own[:1])
    start(k_other)
    received(v_own[:1])
    start(v_other)
    wait(here_q)
    received(q_even)
    received(k_own[1:])
    received(k_other)

    def row_place(r):
        return lax.rem(x - r // OWN + NX, NX) * (NZ * OWN) + z * OWN + lax.rem(r, OWN)

    def slot_of(linear):
        rest = lax.rem(linear, PLANE)
        return (linear // PLANE) * PLANE + lax.rem(rest // OWN, NZ) * HALF + (rest // (NZ * OWN)) * OWN + lax.rem(rest, OWN)

    def is_two(r):
        a = y * PLANE + row_place(r)
        sought = lax.rem(a + 2, BLOCKS)
        hit = 0
        for k in range(LISTED):
            hit = jnp.where(key_blocks[k, x, a] == sought, 1, hit)
        return hit

    def slots(r):
        linear = PLANE + row_place(r)
        fixed = [slot_of(linear + o) for o in FIXED]
        either = [(slot_of(linear + two), slot_of(linear + three)) for two, three in EITHER]
        two = is_two(r)
        picks = fixed + [jnp.where(two == 1, p, q) for p, q in either]
        weight = two.astype(f32)

        def add(acc, k, part):
            if k < len(FIXED):
                acc[fixed[k]] += part
            else:
                p, q = either[k - len(FIXED)]
                acc[p] += part * weight
                acc[q] += part * (1.0 - weight)

        return picks, add

    def heads_of(array, r):
        return jnp.concatenate([array[r, :, h * HD : (h + 1) * HD] for h in range(PER)], 0)

    def folded(array):
        return array.reshape(BLOCK // 8, 8, WIDE)

    def scores(r):
        q = heads_of(q_all, r)
        picks, _ = slots(r)
        high = None
        for k in range(LISTED):
            s = dot(kw[picks[k]], q, 1, 1) * scale_two
            s_all[r, k] = s
            top = folded(s).max(0)
            high = top if high is None else jnp.maximum(high, top)
        high = high.max(0, keepdims=True)
        total = jnp.zeros((8, WIDE), f32)
        for k in range(LISTED):
            total = total + folded(jnp.exp2(s_all[r, k] - high)).sum(0)
        log_total = jnp.log(total.sum(0, keepdims=True)) * LOG2E
        shift_all[r] = jnp.broadcast_to(high + log_total, (8, WIDE))

    def even_scores(i, _):
        scores(i * OWN)
        return 0

    def odd_scores(i, _):
        scores(i * OWN + 1)
        return 0

    lax.fori_loop(0, NX, even_scores, 0)
    received(q_odd)
    lax.fori_loop(0, NX, odd_scores, 0)
    wait(here_g)
    received(g_x)
    received(v_own[1:])
    received(v_other)

    def back(r, which, out, local):
        d, half = r // OWN, lax.rem(r, OWN)
        dst = columns(out, half, x, WIDE)
        n = which * ROWS + r
        if local:
            return pltpu.make_async_copy(od.at[r, which], dst, od_recv.at[n])
        return remote(od.at[r, which], dst, od_send.at[n], od_recv.at[n], at(0, NX - d, 0))

    def send_back(r, which, out, result):
        for h in range(PER):
            od[r, which, :, h * HD : (h + 1) * HD] = result[h * BLOCK : (h + 1) * BLOCK].astype(bf16)

        @pl.when(r < OWN)
        def _():
            back(r, which, out, True).start()

        @pl.when(r >= OWN)
        def _():
            back(r, which, out, False).start()

    def outputs(step, _):
        r = lax.rem(step + OWN, ROWS)
        g = heads_of(g_all, r)
        picks, add = slots(r)
        shift = shift_all[r, 0:1]
        o = None
        for k in range(LISTED):
            p = jnp.exp2(s_all[r, k] - shift).astype(bf16)
            add(dv_acc, k, dot(p, g, 1, 0))
            part = dot(p, vw[picks[k]], 0, 0)
            o = part if o is None else o + part
        send_back(r, 0, attended, o)
        row_dot = (g.astype(f32) * o).sum(-1, keepdims=True)
        dot_all[r] = jnp.broadcast_to(row_dot, (WIDE, HD)).T[0:8]
        return 0

    lax.fori_loop(0, ROWS, outputs, 0)

    accs = (dv_acc, dk_acc)
    outs = (value_grad, key_grad)

    def y_copy(kv, half, part, side):
        n = ((kv * 2 + half) * PARTS + part) * 2 + side
        return remote(stage.at[n], arrived.at[n], y_send.at[n], y_recv.at[n], at(3 if side == 0 else 1, 0, 0))

    def z_copy(kv, part):
        n = kv * PARTS + part
        return remote(z_stage.at[n], z_arrived.at[n], z_send.at[n], z_recv.at[n], at(0, 0, 1))

    def x_copy(kv, to, m, local):
        src = final.at[kv, to * OWN + m]
        dst = columns(outs[kv], m, x, HD)
        n = (kv * NX + x) * OWN + m
        if local:
            return pltpu.make_async_copy(src, dst, x_recv.at[n])
        return remote(src, dst, x_send.at[(kv * NX + to) * OWN + m], x_recv.at[n], {"ctx": index_of(y, to, z)})

    def x_arrival(kv, d, m):
        dst = columns(outs[kv], m, lax.rem(x + d, NX), HD)
        n = (kv * NX + lax.rem(x + d, NX)) * OWN + m
        return remote(final.at[kv, m], dst, x_send.at[n], x_recv.at[n], at(0, d, 0))

    def both(kv, half, part):
        return [y_copy(kv, half, part, side) for side in range(2)]

    def to_y(kv):
        for half in range(2):
            for part in range(PARTS):
                for side in range(2):
                    begin = side * 2 * PLANE + (1 - z if half == 0 else z) * HALF + part * CHUNK
                    stage[((kv * 2 + half) * PARTS + part) * 2 + side] = accs[kv][pl.ds(begin, CHUNK)].astype(bf16)
                    y_copy(kv, half, part, side).start()

    def collected(kv, half, part, begin):
        received(both(kv, half, part))
        n = ((kv * 2 + half) * PARTS + part) * 2
        summed = accs[kv][pl.ds(begin + part * CHUNK, CHUNK)]
        return summed + arrived[n].astype(f32) + arrived[n + 1].astype(f32)

    def to_z(kv, part):
        z_stage[kv * PARTS + part] = collected(kv, 0, part, other_half).astype(bf16)
        z_copy(kv, part).start()

    def to_x(kv, part):
        summed = collected(kv, 1, part, near_half)
        z_copy(kv, part).wait_recv()
        summed = summed + z_arrived[kv * PARTS + part].astype(f32)
        final[kv, part * CHUNK : (part + 1) * CHUNK] = summed.astype(bf16)
        for i in range(CHUNK // OWN):
            to = part * (CHUNK // OWN) + i

            @pl.when(to == x)
            def _():
                for m in range(OWN):
                    x_copy(kv, to, m, True).start()

            @pl.when(to != x)
            def _():
                for m in range(OWN):
                    x_copy(kv, to, m, False).start()

    to_y(0)
    tau_acc[...] = jnp.zeros_like(tau_acc)

    def score_grads(step, _):
        @pl.when(step == 5)
        def _():
            for part in range(PARTS):
                to_z(0, part)

        r = step
        q = heads_of(q_all, r)
        g = heads_of(g_all, r)
        picks, add = slots(r)
        row_dot = dot_all[r, 0:1]
        shift = shift_all[r, 0:1]
        tau = jnp.zeros((8, WIDE), f32)
        for k in range(LISTED):
            s = s_all[r, k]
            t = jnp.exp2(s - shift) * (dot(vw[picks[k]], g, 1, 1) - row_dot)
            tau = tau + folded(t * s).sum(0)
            ds_all[r, k] = (t * scale).astype(bf16)
        for k in range(LISTED):
            add(dk_acc, k, dot(ds_all[r, k], q, 1, 0))
        tau_acc[...] += tau / scale_two
        return 0

    lax.fori_loop(0, ROWS, score_grads, 0)
    to_y(1)

    parts = jnp.concatenate([tau_acc[:, h * BLOCK : (h + 1) * BLOCK].sum(0, keepdims=True) for h in range(PER)], 0)
    tau_x[x] = jnp.concatenate([parts, jnp.zeros_like(parts)], 0)
    tau_first = [remote(tau_x.at[x], tau_x.at[x], tau_send.at[d - 1], tau_recv.at[d - 1], at(0, d, 0)) for d in (1, 2, 3)]
    start(tau_first)

    def query_grads(step, _):
        r = lax.rem(step + OWN, ROWS)
        picks, _ = slots(r)
        dq = None
        for k in range(LISTED):
            part = dot(ds_all[r, k], kw[picks[k]], 0, 0)
            dq = part if dq is None else dq + part
        send_back(r, 1, query_grad, dq)
        return 0

    lax.fori_loop(0, ROWS // 2, query_grads, 0)
    to_z(1, 0)
    lax.fori_loop(ROWS // 2, ROWS, query_grads, 0)
    for part in range(1, PARTS):
        to_z(1, part)
    for part in range(PARTS):
        to_x(0, part)
    received(tau_first)
    tau_y[y] = tau_x[...]
    tau_second = [remote(tau_y.at[y], tau_y.at[y], tau_send.at[d + 2], tau_recv.at[d + 2], at(d, 0, 0)) for d in (1, 2, 3)]
    start(tau_second)
    received(tau_second)
    spot = z * BATCH + batch
    tau_z[spot] = tau_y[0] + tau_y[1] + tau_y[2] + tau_y[3]
    tau_third = []
    for dz in range(NZ):
        for db in range(BATCH):
            if dz or db:
                n = 6 + len(tau_third)
                tau_third.append(remote(tau_z.at[spot], tau_z.at[spot], tau_send.at[n], tau_recv.at[n], far(dz, db)))
    start(tau_third)
    for part in range(PARTS):
        to_x(1, part)
    received(tau_third)
    whole = tau_z[0]
    for n in range(1, NZ * BATCH):
        whole = whole + tau_z[n]
    norm = math.sqrt(HD) * math.sqrt(BATCH * NY * NX * NZ * TOKENS)
    for n in range(NX):
        for h in range(PER):
            tau_out[n * PER + h] = jnp.sum(whole[n, h : h + 1, :]) / norm

    for which, out in enumerate((attended, query_grad)):
        for r in range(ROWS):
            back(r, which, out, r < OWN).wait()
    for kv in range(2):
        for m in range(OWN):
            x_copy(kv, x, m, True).wait()
            for d in (1, 2, 3):
                x_arrival(kv, d, m).wait_recv()
                x_copy(kv, lax.rem(x + d, NX), m, False).wait_send()
        for part in range(PARTS):
            z_copy(kv, part).wait_send()
            for half in range(2):
                for copy in both(kv, half, part):
                    copy.wait_send()
    for copy in k_x + v_x + q_x + g_x + k_own + k_other + v_own + v_other + tau_first + tau_second + tau_third:
        copy.wait_send()


def copy_out(*refs):
    n = (len(refs) - 2) // 3
    sources, results, held = refs[:n], refs[n : 2 * n], refs[2 * n : 3 * n]
    in_sem, out_sem = refs[3 * n :]
    pieces = [(i, m) for i in range(n) for m in range(OWN if i < n - 1 else 1)]

    def piece(ref, i, m):
        return ref.at[m] if i < n - 1 else ref

    into = [pltpu.make_async_copy(piece(sources[i], i, m), piece(held[i], i, m), in_sem.at[j]) for j, (i, m) in enumerate(pieces)]
    away = [pltpu.make_async_copy(piece(held[i], i, m), piece(results[i], i, m), out_sem.at[j]) for j, (i, m) in enumerate(pieces)]
    for copy in into:
        copy.start()
    for first, second in zip(into, away):
        first.wait()
        second.start()
    for copy in away:
        copy.wait()


def body(queries, keys, values, tau, out_grad, key_blocks):
    anywhere = pl.BlockSpec(memory_space=pl.ANY)
    scalars = pl.BlockSpec(memory_space=pltpu.SMEM)
    shape = lambda a: (OWN, BLOCK, a.shape[2])
    chunk = (CHUNK, BLOCK, HD)
    blocked = [a.reshape(shape(a)) for a in (queries, keys, values, out_grad)]
    outs = pl.pallas_call(
        kernel,
        name="attention",
        out_shape=(
            jax.ShapeDtypeStruct(shape(queries), bf16),
            jax.ShapeDtypeStruct(shape(queries), bf16),
            jax.ShapeDtypeStruct(shape(keys), bf16),
            jax.ShapeDtypeStruct(shape(keys), bf16),
            jax.ShapeDtypeStruct((HEADS,), f32),
        ),
        in_specs=[scalars, scalars] + [anywhere] * 4,
        out_specs=(anywhere,) * 4 + (scalars,),
        scratch_shapes=[
            pltpu.VMEM((WINDOW, BLOCK, HD), bf16),
            pltpu.VMEM((WINDOW, BLOCK, HD), bf16),
            pltpu.VMEM((ROWS, BLOCK, WIDE), bf16),
            pltpu.VMEM((ROWS, BLOCK, WIDE), bf16),
            pltpu.VMEM((ROWS, LISTED, BLOCK, WIDE), f32),
            pltpu.VMEM((ROWS, LISTED, BLOCK, WIDE), bf16),
            pltpu.VMEM((ROWS, 8, WIDE), f32),
            pltpu.VMEM((ROWS, 8, WIDE), f32),
            pltpu.VMEM((WINDOW, BLOCK, HD), f32),
            pltpu.VMEM((WINDOW, BLOCK, HD), f32),
            pltpu.VMEM((ROWS, 2, BLOCK, WIDE), bf16),
            pltpu.VMEM((8 * PARTS,) + chunk, bf16),
            pltpu.VMEM((8 * PARTS,) + chunk, bf16),
            pltpu.VMEM((2 * PARTS,) + chunk, bf16),
            pltpu.VMEM((2 * PARTS,) + chunk, bf16),
            pltpu.VMEM((2, HALF, BLOCK, HD), bf16),
            pltpu.VMEM((8, WIDE), f32),
            pltpu.VMEM((NX, 8, BLOCK), f32),
            pltpu.VMEM((NY, NX, 8, BLOCK), f32),
            pltpu.VMEM((NZ * BATCH, NX, 8, BLOCK), f32),
            pltpu.SemaphoreType.DMA((8,)),
            pltpu.SemaphoreType.DMA((34,)),
            pltpu.SemaphoreType.DMA((34,)),
            pltpu.SemaphoreType.DMA((2 * ROWS,)),
            pltpu.SemaphoreType.DMA((2 * ROWS,)),
            pltpu.SemaphoreType.DMA((8 * PARTS,)),
            pltpu.SemaphoreType.DMA((8 * PARTS,)),
            pltpu.SemaphoreType.DMA((2 * PARTS,)),
            pltpu.SemaphoreType.DMA((2 * PARTS,)),
            pltpu.SemaphoreType.DMA((2 * NX * OWN,)),
            pltpu.SemaphoreType.DMA((2 * NX * OWN,)),
            pltpu.SemaphoreType.DMA((13,)),
            pltpu.SemaphoreType.DMA((13,)),
        ],
        compiler_params=pltpu.CompilerParams(
            collective_id=0, has_side_effects=True, vmem_limit_bytes=62 << 20
        ),
    )(key_blocks.transpose(2, 0, 1), tau, *blocked)
    outs = pl.pallas_call(
        copy_out,
        name="copy_out",
        out_shape=tuple(jax.ShapeDtypeStruct(o.shape, o.dtype) for o in outs),
        in_specs=[anywhere] * len(outs),
        out_specs=(anywhere,) * len(outs),
        scratch_shapes=[pltpu.VMEM(o.shape, o.dtype) for o in outs] + [pltpu.SemaphoreType.DMA((9,))] * 2,
    )(*outs)
    return tuple(o.reshape(a.shape) for o, a in zip(outs[:4], (queries, queries, keys, keys))) + (outs[4],)


def solution(mesh):
    sharded = P("batch", "ctx", None)
    return jax.shard_map(
        body,
        mesh=mesh,
        in_specs=(sharded, sharded, sharded, P(), sharded, P()),
        out_specs=(sharded, sharded, sharded, sharded, P()),
        check_vma=False,
    )
```

```python
import math

import jax
import jax.numpy as jnp
from jax import lax
from jax.experimental import pallas as pl
from jax.experimental.pallas import tpu as pltpu
from jax.sharding import PartitionSpec as P

HEADS = 16
GROUPS = 4
PER = HEADS // GROUPS
HD = 128
BLOCK = 128
BLOCKS = 64
WIDE = PER * HD
NY, NX, NZ = 4, 4, 2
OWN = 2
ROWS = NX * OWN
HALF = NX * OWN
PLANE = NZ * HALF
WINDOW = 3 * PLANE
PARTS = 2
CHUNK = HALF // PARTS
TOKENS = OWN * BLOCK
FIXED = (-1, 0, 1, 6, -6)
EITHER = ((2, 3), (-2, -3), (4, 9), (-4, -9), (8, 12), (-8, -12), (10, 15), (-10, -15))
LISTED = len(FIXED) + len(EITHER)
f32 = jnp.float32
bf16 = jnp.bfloat16
LOG2E = math.log2(math.e)
MESH = pl.DeviceIdType.MESH
BATCH = 4


def index_of(y, x, z):
    return lax.rem(y + NY, NY) * (NX * NZ) + lax.rem(x + NX, NX) * NZ + lax.rem(z, NZ)


def dot(a, b, ca, cb):
    return lax.dot_general(a, b, (((ca,), (cb,)), ((), ())), preferred_element_type=f32)


def kernel(
    key_blocks, tau_ref, queries, keys, values, grads,
    attended, query_grad, key_grad, value_grad, tau_out,
    kw, vw, q_all, g_all, s_all, ds_all, shift_all, dot_all, dk_acc, dv_acc, od,
    stage, arrived, z_stage, z_arrived, final, tau_acc, tau_x, tau_y, tau_z,
    here_sem, in_send, in_recv, od_send, od_recv, y_send, y_recv, z_send, z_recv, x_send, x_recv, tau_send, tau_recv,
):
    me = lax.axis_index("ctx")
    batch = lax.axis_index("batch")
    y, x, z = me // (NX * NZ), lax.rem(me // NZ, NX), lax.rem(me, NZ)

    def at(dy, dx, dz):
        return {"ctx": index_of(y + dy, x + dx, z + dz)}

    def far(dz, db):
        return {"ctx": index_of(y, x, z + dz), "batch": lax.rem(batch + db, BATCH)}

    def remote(src, dst, send, recv, device):
        return pltpu.make_async_remote_copy(
            src_ref=src, dst_ref=dst, send_sem=send, recv_sem=recv,
            device_id=device, device_id_type=MESH,
        )

    near_half = PLANE + z * HALF
    other_half = PLANE + (1 - z) * HALF

    def columns(array, n, place, width):
        return array.at[n, :, pl.ds(pl.multiple_of(place * width, width), width)]

    here_k, here_v, here_q, here_g = [
        [
            pltpu.make_async_copy(columns(array, n, x, width), place(0, n), here_sem.at[2 * i + n])
            for n in range(OWN)
        ]
        for i, (array, width, place) in enumerate(
            (
                (keys, HD, lambda d, n: kw.at[near_half + x * OWN + n]),
                (values, HD, lambda d, n: vw.at[near_half + x * OWN + n]),
                (queries, WIDE, lambda d, n: q_all.at[d * OWN + n]),
                (grads, WIDE, lambda d, n: g_all.at[d * OWN + n]),
            )
        )
    ]
    here = here_k + here_v + here_q + here_g
    for copy in here:
        copy.start()

    partners = [at(0, d, 0) for d in (1, 2, 3)] + [at(d, 0, 0) for d in (1, 2, 3)]
    partners += [far(dz, db) for dz in range(NZ) for db in range(BATCH) if dz or db]
    barrier = pltpu.get_barrier_semaphore()
    for device in partners:
        pl.semaphore_signal(barrier, inc=1, device_id=device, device_id_type=MESH)
    pl.semaphore_wait(barrier, len(partners))

    def along_x(array, width, place, first):
        out = []
        for d in (1, 2, 3):
            to = lax.rem(x + d, NX)
            for n in range(OWN):
                i = first + (d - 1) * OWN + n
                out.append(
                    remote(columns(array, n, to, width), place(d, n), in_send.at[i], in_recv.at[i], at(0, d, 0))
                )
        return out

    k_x = along_x(keys, HD, lambda d, n: kw.at[near_half + x * OWN + n], 0)
    v_x = along_x(values, HD, lambda d, n: vw.at[near_half + x * OWN + n], 6)
    q_x = along_x(queries, WIDE, lambda d, n: q_all.at[d * OWN + n], 12)
    g_x = along_x(grads, WIDE, lambda d, n: g_all.at[d * OWN + n], 18)

    def reached(half, part, side):
        low, high = part * CHUNK, (part + 1) * CHUNK
        if half == 1 and side == 0:
            low = max(low, 1)
        if half == 1 and side == 1:
            high = min(high, HALF - 1)
        return low, high - low

    def plane_sends(window, n):
        to_z, to_y = [], []
        for part in range(PARTS):
            span = window.at[pl.ds(near_half + part * CHUNK, CHUNK)]
            to_z.append(remote(span, span, in_send.at[n], in_recv.at[n], at(0, 0, 1)))
            n += 1
        for half, begin in ((1, near_half), (0, other_half)):
            to_y.append([])
            for part in range(PARTS):
                pair = []
                for side in range(2):
                    low, count = reached(half, part, side)
                    src = window.at[pl.ds(begin + low, count)]
                    dst = window.at[pl.ds(begin + low + (PLANE if side else -PLANE), count)]
                    pair.append(remote(src, dst, in_send.at[n], in_recv.at[n], at(3 if side else 1, 0, 0)))
                    n += 1
                to_y[-1].append(pair)
        return to_z, to_y[0], to_y[1]

    k_z, k_own, k_other = plane_sends(kw, 24)
    v_z, v_own, v_other = plane_sends(vw, 24 + 5 * PARTS)

    def start(copies):
        for copy in copies:
            copy.start()

    def received(copies):
        for copy in copies:
            copy.wait_recv()

    def wait(copies):
        for copy in copies:
            copy.wait()

    def flat(pairs):
        return [copy for pair in pairs for copy in pair]

    q_even, q_odd = q_x[0::OWN], q_x[1::OWN]
    g_even, g_odd = g_x[0::OWN], g_x[1::OWN]
    for copies in (k_x, v_x, q_even, q_odd, g_even, g_odd):
        start(copies)
    dk_acc[...] = jnp.zeros_like(dk_acc)
    dv_acc[...] = jnp.zeros_like(dv_acc)
    for window in (kw, vw):
        for end in (z * HALF, 2 * PLANE + z * HALF + HALF - 1):
            window[end] = jnp.zeros((BLOCK, HD), bf16)
    scale = jnp.concatenate(
        [jnp.full((1, BLOCK), tau_ref[x * PER + h] / math.sqrt(HD), f32) for h in range(PER)], 1
    )
    scale_two = scale * LOG2E
    wait(here_k)
    received(k_x)
    start(k_z)
    start(flat(k_own))
    wait(here_v)
    received(v_x)
    start(v_z)
    for part in range(PARTS):
        received(k_z[part : part + 1])
        start(k_other[part])
    start(flat(v_own))
    wait(here_q)
    received(q_even)
    received(flat(k_own))
    for part in range(PARTS):
        received(v_z[part : part + 1])
        start(v_other[part])
    received(flat(k_other))

    def row_place(r):
        return lax.rem(x - r // OWN + NX, NX) * (NZ * OWN) + z * OWN + lax.rem(r, OWN)

    def slot_of(linear):
        rest = lax.rem(linear, PLANE)
        return (linear // PLANE) * PLANE + lax.rem(rest // OWN, NZ) * HALF + (rest // (NZ * OWN)) * OWN + lax.rem(rest, OWN)

    def is_two(r):
        a = y * PLANE + row_place(r)
        sought = lax.rem(a + 2, BLOCKS)
        hit = 0
        for k in range(LISTED):
            hit = jnp.where(key_blocks[k, x, a] == sought, 1, hit)
        return hit

    def slots(r):
        linear = PLANE + row_place(r)
        fixed = [slot_of(linear + o) for o in FIXED]
        either = [(slot_of(linear + two), slot_of(linear + three)) for two, three in EITHER]
        two = is_two(r)
        picks = fixed + [jnp.where(two == 1, p, q) for p, q in either]
        weight = two.astype(f32)

        def add(acc, k, part):
            if k < len(FIXED):
                acc[fixed[k]] += part
            else:
                p, q = either[k - len(FIXED)]
                acc[p] += part * weight
                acc[q] += part * (1.0 - weight)

        return picks, add

    def heads_of(array, r):
        return jnp.concatenate([array[r, :, h * HD : (h + 1) * HD] for h in range(PER)], 0)

    def folded(array):
        return array.reshape(BLOCK // 8, 8, WIDE)

    def scores(r):
        q = heads_of(q_all, r)
        picks, _ = slots(r)
        high = None
        for k in range(LISTED):
            s = dot(kw[picks[k]], q, 1, 1) * scale_two
            s_all[r, k] = s
            top = folded(s).max(0)
            high = top if high is None else jnp.maximum(high, top)
        high = high.max(0, keepdims=True)
        total = jnp.zeros((8, WIDE), f32)
        for k in range(LISTED):
            total = total + folded(jnp.exp2(s_all[r, k] - high)).sum(0)
        log_total = jnp.log(total.sum(0, keepdims=True)) * LOG2E
        shift_all[r] = jnp.broadcast_to(high + log_total, (8, WIDE))

    def even_scores(i, _):
        scores(i * OWN)
        return 0

    def odd_scores(i, _):
        scores(i * OWN + 1)
        return 0

    lax.fori_loop(0, NX, even_scores, 0)
    received(q_odd)
    lax.fori_loop(0, NX, odd_scores, 0)
    wait(here_g)
    received(g_even)
    received(flat(v_own))
    received(flat(v_other))

    def back(r, which, out, local):
        d, half = r // OWN, lax.rem(r, OWN)
        dst = columns(out, half, x, WIDE)
        n = which * ROWS + r
        if local:
            return pltpu.make_async_copy(od.at[r, which], dst, od_recv.at[n])
        return remote(od.at[r, which], dst, od_send.at[n], od_recv.at[n], at(0, NX - d, 0))

    def send_back(r, which, out, result):
        for h in range(PER):
            od[r, which, :, h * HD : (h + 1) * HD] = result[h * BLOCK : (h + 1) * BLOCK].astype(bf16)

        @pl.when(r < OWN)
        def _():
            back(r, which, out, True).start()

        @pl.when(r >= OWN)
        def _():
            back(r, which, out, False).start()

    def outputs(step, _):
        r = lax.rem(step + 1, NX) * OWN + step // NX

        @pl.when(step == NX)
        def _():
            received(g_odd)

        g = heads_of(g_all, r)
        picks, add = slots(r)
        shift = shift_all[r, 0:1]
        o = None
        for k in range(LISTED):
            p = jnp.exp2(s_all[r, k] - shift).astype(bf16)
            add(dv_acc, k, dot(p, g, 1, 0))
            part = dot(p, vw[picks[k]], 0, 0)
            o = part if o is None else o + part
        send_back(r, 0, attended, o)
        row_dot = (g.astype(f32) * o).sum(-1, keepdims=True)
        dot_all[r] = jnp.broadcast_to(row_dot, (WIDE, HD)).T[0:8]
        return 0

    lax.fori_loop(0, ROWS, outputs, 0)

    accs = (dv_acc, dk_acc)
    outs = (value_grad, key_grad)

    def y_copy(kv, half, part, side):
        n = ((kv * 2 + half) * PARTS + part) * 2 + side
        span = pl.ds(0, reached(half, part, side)[1])
        return remote(stage.at[n, span], arrived.at[n, span], y_send.at[n], y_recv.at[n], at(3 if side == 0 else 1, 0, 0))

    def z_copy(kv, part):
        n = kv * PARTS + part
        return remote(z_stage.at[n], z_arrived.at[n], z_send.at[n], z_recv.at[n], at(0, 0, 1))

    def x_copy(kv, to, m, local):
        src = final.at[kv, to * OWN + m]
        dst = columns(outs[kv], m, x, HD)
        n = (kv * NX + x) * OWN + m
        if local:
            return pltpu.make_async_copy(src, dst, x_recv.at[n])
        return remote(src, dst, x_send.at[(kv * NX + to) * OWN + m], x_recv.at[n], {"ctx": index_of(y, to, z)})

    def x_arrival(kv, d, m):
        dst = columns(outs[kv], m, lax.rem(x + d, NX), HD)
        n = (kv * NX + lax.rem(x + d, NX)) * OWN + m
        return remote(final.at[kv, m], dst, x_send.at[n], x_recv.at[n], at(0, d, 0))

    def both(kv, half, part):
        return [y_copy(kv, half, part, side) for side in range(2)]

    def to_y(kv):
        for half in range(2):
            for part in range(PARTS):
                for side in range(2):
                    low, count = reached(half, part, side)
                    begin = side * 2 * PLANE + (1 - z if half == 0 else z) * HALF + low
                    n = ((kv * 2 + half) * PARTS + part) * 2 + side
                    stage[n, :count] = accs[kv][pl.ds(begin, count)].astype(bf16)
                    y_copy(kv, half, part, side).start()

    def collected(kv, half, part, begin):
        received(both(kv, half, part))
        for side in range(2):
            low, count = reached(half, part, side)
            n = ((kv * 2 + half) * PARTS + part) * 2 + side
            accs[kv][pl.ds(begin + low, count)] += arrived[n, :count].astype(f32)
        return accs[kv][pl.ds(begin + part * CHUNK, CHUNK)]

    def to_z(kv, part):
        z_stage[kv * PARTS + part] = collected(kv, 0, part, other_half).astype(bf16)
        z_copy(kv, part).start()

    def to_x(kv, part):
        summed = collected(kv, 1, part, near_half)
        z_copy(kv, part).wait_recv()
        summed = summed + z_arrived[kv * PARTS + part].astype(f32)
        final[kv, part * CHUNK : (part + 1) * CHUNK] = summed.astype(bf16)
        for i in range(CHUNK // OWN):
            to = part * (CHUNK // OWN) + i

            @pl.when(to == x)
            def _():
                for m in range(OWN):
                    x_copy(kv, to, m, True).start()

            @pl.when(to != x)
            def _():
                for m in range(OWN):
                    x_copy(kv, to, m, False).start()

    to_y(0)
    tau_acc[...] = jnp.zeros_like(tau_acc)

    def score_grads(step, _):
        @pl.when(step == 5)
        def _():
            for part in range(PARTS):
                to_z(0, part)

        r = step
        q = heads_of(q_all, r)
        g = heads_of(g_all, r)
        picks, add = slots(r)
        row_dot = dot_all[r, 0:1]
        shift = shift_all[r, 0:1]
        tau = jnp.zeros((8, WIDE), f32)
        for k in range(LISTED):
            s = s_all[r, k]
            t = jnp.exp2(s - shift) * (dot(vw[picks[k]], g, 1, 1) - row_dot)
            tau = tau + folded(t * s).sum(0)
            ds_all[r, k] = (t * scale).astype(bf16)
        for k in range(LISTED):
            add(dk_acc, k, dot(ds_all[r, k], q, 1, 0))
        tau_acc[...] += tau / scale_two
        return 0

    lax.fori_loop(0, ROWS, score_grads, 0)
    to_y(1)

    parts = jnp.concatenate([tau_acc[:, h * BLOCK : (h + 1) * BLOCK].sum(0, keepdims=True) for h in range(PER)], 0)
    tau_x[x] = jnp.concatenate([parts, jnp.zeros_like(parts)], 0)
    tau_first = [remote(tau_x.at[x], tau_x.at[x], tau_send.at[d - 1], tau_recv.at[d - 1], at(0, d, 0)) for d in (1, 2, 3)]
    start(tau_first)

    def query_grads(step, _):
        r = lax.rem(step + OWN, ROWS)
        picks, _ = slots(r)
        dq = None
        for k in range(LISTED):
            part = dot(ds_all[r, k], kw[picks[k]], 0, 0)
            dq = part if dq is None else dq + part
        send_back(r, 1, query_grad, dq)
        return 0

    lax.fori_loop(0, ROWS // 2, query_grads, 0)
    to_z(1, 0)
    lax.fori_loop(ROWS // 2, ROWS, query_grads, 0)
    for part in range(1, PARTS):
        to_z(1, part)
    for part in range(PARTS):
        to_x(0, part)
    received(tau_first)
    tau_y[y] = tau_x[...]
    tau_second = [remote(tau_y.at[y], tau_y.at[y], tau_send.at[d + 2], tau_recv.at[d + 2], at(d, 0, 0)) for d in (1, 2, 3)]
    start(tau_second)
    received(tau_second)
    spot = z * BATCH + batch
    tau_z[spot] = tau_y[0] + tau_y[1] + tau_y[2] + tau_y[3]
    tau_third = []
    for dz in range(NZ):
        for db in range(BATCH):
            if dz or db:
                n = 6 + len(tau_third)
                tau_third.append(remote(tau_z.at[spot], tau_z.at[spot], tau_send.at[n], tau_recv.at[n], far(dz, db)))
    start(tau_third)
    for part in range(PARTS):
        to_x(1, part)
    received(tau_third)
    whole = tau_z[0]
    for n in range(1, NZ * BATCH):
        whole = whole + tau_z[n]
    norm = math.sqrt(HD) * math.sqrt(BATCH * NY * NX * NZ * TOKENS)
    for n in range(NX):
        for h in range(PER):
            tau_out[n * PER + h] = jnp.sum(whole[n, h : h + 1, :]) / norm

    for which, out in enumerate((attended, query_grad)):
        for r in range(ROWS):
            back(r, which, out, r < OWN).wait()
    for kv in range(2):
        for m in range(OWN):
            x_copy(kv, x, m, True).wait()
            for d in (1, 2, 3):
                x_arrival(kv, d, m).wait_recv()
                x_copy(kv, lax.rem(x + d, NX), m, False).wait_send()
        for part in range(PARTS):
            z_copy(kv, part).wait_send()
            for half in range(2):
                for copy in both(kv, half, part):
                    copy.wait_send()
    for copy in k_x + v_x + q_x + g_x + k_z + v_z + flat(k_own + k_other + v_own + v_other) + tau_first + tau_second + tau_third:
        copy.wait_send()


def copy_out(*refs):
    n = (len(refs) - 2) // 3
    sources, results, held = refs[:n], refs[n : 2 * n], refs[2 * n : 3 * n]
    in_sem, out_sem = refs[3 * n :]
    pieces = [(i, m) for i in range(n) for m in range(OWN if i < n - 1 else 1)]

    def piece(ref, i, m):
        return ref.at[m] if i < n - 1 else ref

    into = [pltpu.make_async_copy(piece(sources[i], i, m), piece(held[i], i, m), in_sem.at[j]) for j, (i, m) in enumerate(pieces)]
    away = [pltpu.make_async_copy(piece(held[i], i, m), piece(results[i], i, m), out_sem.at[j]) for j, (i, m) in enumerate(pieces)]
    for copy in into:
        copy.start()
    for first, second in zip(into, away):
        first.wait()
        second.start()
    for copy in away:
        copy.wait()


def body(queries, keys, values, tau, out_grad, key_blocks):
    anywhere = pl.BlockSpec(memory_space=pl.ANY)
    scalars = pl.BlockSpec(memory_space=pltpu.SMEM)
    shape = lambda a: (OWN, BLOCK, a.shape[2])
    chunk = (CHUNK, BLOCK, HD)
    blocked = [a.reshape(shape(a)) for a in (queries, keys, values, out_grad)]
    outs = pl.pallas_call(
        kernel,
        name="attention",
        out_shape=(
            jax.ShapeDtypeStruct(shape(queries), bf16),
            jax.ShapeDtypeStruct(shape(queries), bf16),
            jax.ShapeDtypeStruct(shape(keys), bf16),
            jax.ShapeDtypeStruct(shape(keys), bf16),
            jax.ShapeDtypeStruct((HEADS,), f32),
        ),
        in_specs=[scalars, scalars] + [anywhere] * 4,
        out_specs=(anywhere,) * 4 + (scalars,),
        scratch_shapes=[
            pltpu.VMEM((WINDOW, BLOCK, HD), bf16),
            pltpu.VMEM((WINDOW, BLOCK, HD), bf16),
            pltpu.VMEM((ROWS, BLOCK, WIDE), bf16),
            pltpu.VMEM((ROWS, BLOCK, WIDE), bf16),
            pltpu.VMEM((ROWS, LISTED, BLOCK, WIDE), f32),
            pltpu.VMEM((ROWS, LISTED, BLOCK, WIDE), bf16),
            pltpu.VMEM((ROWS, 8, WIDE), f32),
            pltpu.VMEM((ROWS, 8, WIDE), f32),
            pltpu.VMEM((WINDOW, BLOCK, HD), f32),
            pltpu.VMEM((WINDOW, BLOCK, HD), f32),
            pltpu.VMEM((ROWS, 2, BLOCK, WIDE), bf16),
            pltpu.VMEM((8 * PARTS,) + chunk, bf16),
            pltpu.VMEM((8 * PARTS,) + chunk, bf16),
            pltpu.VMEM((2 * PARTS,) + chunk, bf16),
            pltpu.VMEM((2 * PARTS,) + chunk, bf16),
            pltpu.VMEM((2, HALF, BLOCK, HD), bf16),
            pltpu.VMEM((8, WIDE), f32),
            pltpu.VMEM((NX, 8, BLOCK), f32),
            pltpu.VMEM((NY, NX, 8, BLOCK), f32),
            pltpu.VMEM((NZ * BATCH, NX, 8, BLOCK), f32),
            pltpu.SemaphoreType.DMA((8,)),
            pltpu.SemaphoreType.DMA((24 + 10 * PARTS,)),
            pltpu.SemaphoreType.DMA((24 + 10 * PARTS,)),
            pltpu.SemaphoreType.DMA((2 * ROWS,)),
            pltpu.SemaphoreType.DMA((2 * ROWS,)),
            pltpu.SemaphoreType.DMA((8 * PARTS,)),
            pltpu.SemaphoreType.DMA((8 * PARTS,)),
            pltpu.SemaphoreType.DMA((2 * PARTS,)),
            pltpu.SemaphoreType.DMA((2 * PARTS,)),
            pltpu.SemaphoreType.DMA((2 * NX * OWN,)),
            pltpu.SemaphoreType.DMA((2 * NX * OWN,)),
            pltpu.SemaphoreType.DMA((13,)),
            pltpu.SemaphoreType.DMA((13,)),
        ],
        compiler_params=pltpu.CompilerParams(
            collective_id=0, has_side_effects=True, vmem_limit_bytes=62 << 20
        ),
    )(key_blocks.transpose(2, 0, 1), tau, *blocked)
    outs = pl.pallas_call(
        copy_out,
        name="copy_out",
        out_shape=tuple(jax.ShapeDtypeStruct(o.shape, o.dtype) for o in outs),
        in_specs=[anywhere] * len(outs),
        out_specs=(anywhere,) * len(outs),
        scratch_shapes=[pltpu.VMEM(o.shape, o.dtype) for o in outs] + [pltpu.SemaphoreType.DMA((9,))] * 2,
    )(*outs)
    return tuple(o.reshape(a.shape) for o, a in zip(outs[:4], (queries, queries, keys, keys))) + (outs[4],)


def solution(mesh):
    sharded = P("batch", "ctx", None)
    return jax.shard_map(
        body,
        mesh=mesh,
        in_specs=(sharded, sharded, sharded, P(), sharded, P()),
        out_specs=(sharded, sharded, sharded, sharded, P()),
        check_vma=False,
    )
```

```python
import math

import jax
import jax.numpy as jnp
from jax import lax
from jax.experimental import pallas as pl
from jax.experimental.pallas import tpu as pltpu
from jax.sharding import PartitionSpec as P

HEADS = 16
GROUPS = 4
PER = HEADS // GROUPS
HD = 128
BLOCK = 128
BLOCKS = 64
WIDE = PER * HD
NY, NX, NZ = 4, 4, 2
OWN = 2
ROWS = NX * OWN
HALF = NX * OWN
PLANE = NZ * HALF
WINDOW = 3 * PLANE
PARTS = 2
CHUNK = HALF // PARTS
TOKENS = OWN * BLOCK
FIXED = (-1, 0, 1, 6, -6)
EITHER = ((2, 3), (-2, -3), (4, 9), (-4, -9), (8, 12), (-8, -12), (10, 15), (-10, -15))
LISTED = len(FIXED) + len(EITHER)
f32 = jnp.float32
bf16 = jnp.bfloat16
LOG2E = math.log2(math.e)
MESH = pl.DeviceIdType.MESH
BATCH = 4


def index_of(y, x, z):
    return lax.rem(y + NY, NY) * (NX * NZ) + lax.rem(x + NX, NX) * NZ + lax.rem(z, NZ)


def dot(a, b, ca, cb):
    return lax.dot_general(a, b, (((ca,), (cb,)), ((), ())), preferred_element_type=f32)


def kernel(
    key_blocks, tau_ref, queries, keys, values, grads,
    attended, query_grad, key_grad, value_grad, tau_out,
    kw, vw, q_all, g_all, s_all, ds_all, shift_all, dot_all, dk_acc, dv_acc, od,
    stage, arrived, z_stage, z_arrived, final, tau_acc, tau_x, tau_y, tau_z,
    here_sem, in_send, in_recv, od_send, od_recv, y_send, y_recv, z_send, z_recv, x_send, x_recv, tau_send, tau_recv,
):
    me = lax.axis_index("ctx")
    batch = lax.axis_index("batch")
    y, x, z = me // (NX * NZ), lax.rem(me // NZ, NX), lax.rem(me, NZ)

    def at(dy, dx, dz):
        return {"ctx": index_of(y + dy, x + dx, z + dz)}

    def far(dz, db):
        return {"ctx": index_of(y, x, z + dz), "batch": lax.rem(batch + db, BATCH)}

    def remote(src, dst, send, recv, device):
        return pltpu.make_async_remote_copy(
            src_ref=src, dst_ref=dst, send_sem=send, recv_sem=recv,
            device_id=device, device_id_type=MESH,
        )

    near_half = PLANE + z * HALF
    other_half = PLANE + (1 - z) * HALF

    def columns(array, n, place, width):
        return array.at[n, :, pl.ds(pl.multiple_of(place * width, width), width)]

    here_k, here_v, here_q, here_g = [
        [
            pltpu.make_async_copy(columns(array, n, x, width), place(0, n), here_sem.at[2 * i + n])
            for n in range(OWN)
        ]
        for i, (array, width, place) in enumerate(
            (
                (keys, HD, lambda d, n: kw.at[near_half + x * OWN + n]),
                (values, HD, lambda d, n: vw.at[near_half + x * OWN + n]),
                (queries, WIDE, lambda d, n: q_all.at[d * OWN + n]),
                (grads, WIDE, lambda d, n: g_all.at[d * OWN + n]),
            )
        )
    ]
    here = here_k + here_v + here_q + here_g
    for copy in here:
        copy.start()

    partners = [at(0, d, 0) for d in (1, 2, 3)] + [at(d, 0, 0) for d in (1, 2, 3)]
    partners += [far(dz, db) for dz in range(NZ) for db in range(BATCH) if dz or db]
    barrier = pltpu.get_barrier_semaphore()
    for device in partners:
        pl.semaphore_signal(barrier, inc=1, device_id=device, device_id_type=MESH)
    pl.semaphore_wait(barrier, len(partners))

    def along_x(array, width, place, first):
        out = []
        for d in (1, 2, 3):
            to = lax.rem(x + d, NX)
            for n in range(OWN):
                i = first + (d - 1) * OWN + n
                out.append(
                    remote(columns(array, n, to, width), place(d, n), in_send.at[i], in_recv.at[i], at(0, d, 0))
                )
        return out

    k_x = along_x(keys, HD, lambda d, n: kw.at[near_half + x * OWN + n], 0)
    v_x = along_x(values, HD, lambda d, n: vw.at[near_half + x * OWN + n], 6)
    q_x = along_x(queries, WIDE, lambda d, n: q_all.at[d * OWN + n], 12)
    g_x = along_x(grads, WIDE, lambda d, n: g_all.at[d * OWN + n], 18)

    def reached(half, part, side):
        low, high = part * CHUNK, (part + 1) * CHUNK
        if half == 1 and side == 0:
            low = max(low, 1)
        if half == 1 and side == 1:
            high = min(high, HALF - 1)
        return low, high - low

    def plane_sends(window, n):
        to_z, to_y = [], []
        for part in range(PARTS):
            span = window.at[pl.ds(near_half + part * CHUNK, CHUNK)]
            to_z.append(remote(span, span, in_send.at[n], in_recv.at[n], at(0, 0, 1)))
            n += 1
        for half, begin in ((1, near_half), (0, other_half)):
            to_y.append([])
            for part in range(PARTS):
                pair = []
                for side in range(2):
                    low, count = reached(half, part, side)
                    src = window.at[pl.ds(begin + low, count)]
                    dst = window.at[pl.ds(begin + low + (PLANE if side else -PLANE), count)]
                    pair.append(remote(src, dst, in_send.at[n], in_recv.at[n], at(3 if side else 1, 0, 0)))
                    n += 1
                to_y[-1].append(pair)
        return to_z, to_y[0], to_y[1]

    k_z, k_own, k_other = plane_sends(kw, 24)
    v_z, v_own, v_other = plane_sends(vw, 24 + 5 * PARTS)

    def start(copies):
        for copy in copies:
            copy.start()

    def received(copies):
        for copy in copies:
            copy.wait_recv()

    def wait(copies):
        for copy in copies:
            copy.wait()

    def flat(pairs):
        return [copy for pair in pairs for copy in pair]

    q_even, q_odd = q_x[0::OWN], q_x[1::OWN]
    g_even, g_odd = g_x[0::OWN], g_x[1::OWN]
    for copies in (k_x, v_x, q_even, q_odd, g_even, g_odd):
        start(copies)
    dk_acc[...] = jnp.zeros_like(dk_acc)
    dv_acc[...] = jnp.zeros_like(dv_acc)
    for window in (kw, vw):
        for end in (z * HALF, 2 * PLANE + z * HALF + HALF - 1):
            window[end] = jnp.zeros((BLOCK, HD), bf16)
    scale = jnp.concatenate(
        [jnp.full((1, BLOCK), tau_ref[x * PER + h] / math.sqrt(HD), f32) for h in range(PER)], 1
    )
    scale_two = scale * LOG2E
    wait(here_k)
    received(k_x)
    start(k_z)
    start(flat(k_own))
    wait(here_v)
    received(v_x)
    start(v_z)
    for part in range(PARTS):
        received(k_z[part : part + 1])
        start(k_other[part])
    start(flat(v_own))
    wait(here_q)
    received(q_even)
    received(flat(k_own))
    for part in range(PARTS):
        received(v_z[part : part + 1])
        start(v_other[part])
    received(flat(k_other))

    def row_at(step):
        return lax.rem(ROWS + ROWS // 2 - OWN * lax.rem(step, NX), ROWS) + step // NX

    def row_place(r):
        return lax.rem(x - r // OWN + NX, NX) * (NZ * OWN) + z * OWN + lax.rem(r, OWN)

    def slot_of(linear):
        rest = lax.rem(linear, PLANE)
        return (linear // PLANE) * PLANE + lax.rem(rest // OWN, NZ) * HALF + (rest // (NZ * OWN)) * OWN + lax.rem(rest, OWN)

    def is_two(r):
        a = y * PLANE + row_place(r)
        sought = lax.rem(a + 2, BLOCKS)
        hit = 0
        for k in range(LISTED):
            hit = jnp.where(key_blocks[k, x, a] == sought, 1, hit)
        return hit

    def slots(r):
        linear = PLANE + row_place(r)
        fixed = [slot_of(linear + o) for o in FIXED]
        either = [(slot_of(linear + two), slot_of(linear + three)) for two, three in EITHER]
        two = is_two(r)
        picks = fixed + [jnp.where(two == 1, p, q) for p, q in either]
        weight = two.astype(f32)

        def add(acc, k, part):
            if k < len(FIXED):
                acc[fixed[k]] += part
            else:
                p, q = either[k - len(FIXED)]
                acc[p] += part * weight
                acc[q] += part * (1.0 - weight)

        return picks, add

    def heads_of(array, r):
        return jnp.concatenate([array[r, :, h * HD : (h + 1) * HD] for h in range(PER)], 0)

    def folded(array, join):
        rows = BLOCK
        while rows > 8:
            rows //= 2
            array = join(array[:rows], array[rows:])
        return array

    def scores(r):
        q = heads_of(q_all, r)
        picks, _ = slots(r)
        high = None
        for k in range(LISTED):
            s = dot(kw[picks[k]], q, 1, 1) * scale_two
            s_all[r, k] = s
            top = folded(s, jnp.maximum)
            high = top if high is None else jnp.maximum(high, top)
        high = high.max(0, keepdims=True)
        total = jnp.zeros((8, WIDE), f32)
        for k in range(LISTED):
            total = total + folded(jnp.exp2(s_all[r, k] - high), jnp.add)
        log_total = jnp.log(total.sum(0, keepdims=True)) * LOG2E
        shift_all[r] = jnp.broadcast_to(high + log_total, (8, WIDE))

    def even_scores(i, _):
        scores(i * OWN)
        return 0

    def odd_scores(i, _):
        scores(i * OWN + 1)
        return 0

    lax.fori_loop(0, NX, even_scores, 0)
    received(q_odd)
    lax.fori_loop(0, NX, odd_scores, 0)
    wait(here_g)
    received(g_even)
    received(flat(v_own))
    received(flat(v_other))

    def back(r, which, out, local):
        d, half = r // OWN, lax.rem(r, OWN)
        dst = columns(out, half, x, WIDE)
        n = which * ROWS + r
        if local:
            return pltpu.make_async_copy(od.at[r, which], dst, od_recv.at[n])
        return remote(od.at[r, which], dst, od_send.at[n], od_recv.at[n], at(0, NX - d, 0))

    def send_back(r, which, out, result):
        for h in range(PER):
            od[r, which, :, h * HD : (h + 1) * HD] = result[h * BLOCK : (h + 1) * BLOCK].astype(bf16)

        @pl.when(r < OWN)
        def _():
            back(r, which, out, True).start()

        @pl.when(r >= OWN)
        def _():
            back(r, which, out, False).start()

    def outputs(step, _):
        r = row_at(step)

        @pl.when(step == NX)
        def _():
            received(g_odd)

        g = heads_of(g_all, r)
        picks, add = slots(r)
        shift = shift_all[r, 0:1]
        o = None
        for k in range(LISTED):
            p = jnp.exp2(s_all[r, k] - shift).astype(bf16)
            add(dv_acc, k, dot(p, g, 1, 0))
            part = dot(p, vw[picks[k]], 0, 0)
            o = part if o is None else o + part
        send_back(r, 0, attended, o)
        row_dot = (g.astype(f32) * o).sum(-1, keepdims=True)
        dot_all[r] = jnp.broadcast_to(row_dot, (WIDE, HD)).T[0:8]
        return 0

    lax.fori_loop(0, ROWS, outputs, 0)

    accs = (dv_acc, dk_acc)
    outs = (value_grad, key_grad)

    def y_copy(kv, half, part, side):
        n = ((kv * 2 + half) * PARTS + part) * 2 + side
        span = pl.ds(0, reached(half, part, side)[1])
        return remote(stage.at[n, span], arrived.at[n, span], y_send.at[n], y_recv.at[n], at(3 if side == 0 else 1, 0, 0))

    def z_copy(kv, part):
        n = kv * PARTS + part
        return remote(z_stage.at[n], z_arrived.at[n], z_send.at[n], z_recv.at[n], at(0, 0, 1))

    def x_copy(kv, to, m, local):
        src = final.at[kv, to * OWN + m]
        dst = columns(outs[kv], m, x, HD)
        n = (kv * NX + x) * OWN + m
        if local:
            return pltpu.make_async_copy(src, dst, x_recv.at[n])
        return remote(src, dst, x_send.at[(kv * NX + to) * OWN + m], x_recv.at[n], {"ctx": index_of(y, to, z)})

    def x_arrival(kv, d, m):
        dst = columns(outs[kv], m, lax.rem(x + d, NX), HD)
        n = (kv * NX + lax.rem(x + d, NX)) * OWN + m
        return remote(final.at[kv, m], dst, x_send.at[n], x_recv.at[n], at(0, d, 0))

    def both(kv, half, part):
        return [y_copy(kv, half, part, side) for side in range(2)]

    def to_y(kv):
        for half in range(2):
            for part in range(PARTS):
                for side in range(2):
                    low, count = reached(half, part, side)
                    begin = side * 2 * PLANE + (1 - z if half == 0 else z) * HALF + low
                    n = ((kv * 2 + half) * PARTS + part) * 2 + side
                    stage[n, :count] = accs[kv][pl.ds(begin, count)].astype(bf16)
                    y_copy(kv, half, part, side).start()

    def collected(kv, half, part, begin):
        received(both(kv, half, part))
        for side in range(2):
            low, count = reached(half, part, side)
            n = ((kv * 2 + half) * PARTS + part) * 2 + side
            accs[kv][pl.ds(begin + low, count)] += arrived[n, :count].astype(f32)
        return accs[kv][pl.ds(begin + part * CHUNK, CHUNK)]

    def to_z(kv, part):
        z_stage[kv * PARTS + part] = collected(kv, 0, part, other_half).astype(bf16)
        z_copy(kv, part).start()

    def to_x(kv, part):
        summed = collected(kv, 1, part, near_half)
        z_copy(kv, part).wait_recv()
        summed = summed + z_arrived[kv * PARTS + part].astype(f32)
        final[kv, part * CHUNK : (part + 1) * CHUNK] = summed.astype(bf16)
        for i in range(CHUNK // OWN):
            to = part * (CHUNK // OWN) + i

            @pl.when(to == x)
            def _():
                for m in range(OWN):
                    x_copy(kv, to, m, True).start()

            @pl.when(to != x)
            def _():
                for m in range(OWN):
                    x_copy(kv, to, m, False).start()

    to_y(0)
    tau_acc[...] = jnp.zeros_like(tau_acc)

    def score_grads(step, _):
        for part in range(PARTS):

            @pl.when(step == 3 + part)
            def _(part=part):
                to_z(0, part)

            @pl.when(step == ROWS - PARTS + part)
            def _(part=part):
                to_x(0, part)

        r = step
        q = heads_of(q_all, r)
        g = heads_of(g_all, r)
        picks, add = slots(r)
        row_dot = dot_all[r, 0:1]
        shift = shift_all[r, 0:1]
        tau = jnp.zeros((8, WIDE), f32)
        for k in range(LISTED):
            s = s_all[r, k]
            t = jnp.exp2(s - shift) * (dot(vw[picks[k]], g, 1, 1) - row_dot)
            tau = tau + folded(t * s, jnp.add)
            ds_all[r, k] = (t * scale).astype(bf16)
        for k in range(LISTED):
            add(dk_acc, k, dot(ds_all[r, k], q, 1, 0))
        tau_acc[...] += tau / scale_two
        return 0

    lax.fori_loop(0, ROWS, score_grads, 0)
    to_y(1)

    parts = jnp.concatenate([tau_acc[:, h * BLOCK : (h + 1) * BLOCK].sum(0, keepdims=True) for h in range(PER)], 0)
    tau_x[x] = jnp.concatenate([parts, jnp.zeros_like(parts)], 0)
    tau_first = [remote(tau_x.at[x], tau_x.at[x], tau_send.at[d - 1], tau_recv.at[d - 1], at(0, d, 0)) for d in (1, 2, 3)]
    start(tau_first)

    def query_grads(step, _):
        r = row_at(step)
        picks, _ = slots(r)
        dq = None
        for k in range(LISTED):
            part = dot(ds_all[r, k], kw[picks[k]], 0, 0)
            dq = part if dq is None else dq + part
        send_back(r, 1, query_grad, dq)
        return 0

    lax.fori_loop(0, ROWS // 2, query_grads, 0)
    received(tau_first)
    tau_y[y] = tau_x[...]
    tau_second = [remote(tau_y.at[y], tau_y.at[y], tau_send.at[d + 2], tau_recv.at[d + 2], at(d, 0, 0)) for d in (1, 2, 3)]
    start(tau_second)
    to_z(1, 0)
    lax.fori_loop(ROWS // 2, ROWS, query_grads, 0)
    for part in range(1, PARTS):
        to_z(1, part)
    received(tau_second)
    spot = z * BATCH + batch
    tau_z[spot] = tau_y[0] + tau_y[1] + tau_y[2] + tau_y[3]
    tau_third = []
    for dz in range(NZ):
        for db in range(BATCH):
            if dz or db:
                n = 6 + len(tau_third)
                tau_third.append(remote(tau_z.at[spot], tau_z.at[spot], tau_send.at[n], tau_recv.at[n], far(dz, db)))
    start(tau_third)
    for part in range(PARTS):
        to_x(1, part)
    received(tau_third)
    whole = tau_z[0]
    for n in range(1, NZ * BATCH):
        whole = whole + tau_z[n]
    norm = math.sqrt(HD) * math.sqrt(BATCH * NY * NX * NZ * TOKENS)
    for n in range(NX):
        for h in range(PER):
            tau_out[n * PER + h] = jnp.sum(whole[n, h : h + 1, :]) / norm

    for which, out in enumerate((attended, query_grad)):
        for r in range(ROWS):
            back(r, which, out, r < OWN).wait()
    for kv in range(2):
        for m in range(OWN):
            x_copy(kv, x, m, True).wait()
            for d in (1, 2, 3):
                x_arrival(kv, d, m).wait_recv()
                x_copy(kv, lax.rem(x + d, NX), m, False).wait_send()
        for part in range(PARTS):
            z_copy(kv, part).wait_send()
            for half in range(2):
                for copy in both(kv, half, part):
                    copy.wait_send()
    for copy in k_x + v_x + q_x + g_x + k_z + v_z + flat(k_own + k_other + v_own + v_other) + tau_first + tau_second + tau_third:
        copy.wait_send()


def copy_out(*refs):
    n = (len(refs) - 2) // 3
    sources, results, held = refs[:n], refs[n : 2 * n], refs[2 * n : 3 * n]
    in_sem, out_sem = refs[3 * n :]
    pieces = [(i, m) for i in range(n) for m in range(OWN if i < n - 1 else 1)]

    def piece(ref, i, m):
        return ref.at[m] if i < n - 1 else ref

    into = [pltpu.make_async_copy(piece(sources[i], i, m), piece(held[i], i, m), in_sem.at[j]) for j, (i, m) in enumerate(pieces)]
    away = [pltpu.make_async_copy(piece(held[i], i, m), piece(results[i], i, m), out_sem.at[j]) for j, (i, m) in enumerate(pieces)]
    for copy in into:
        copy.start()
    for first, second in zip(into, away):
        first.wait()
        second.start()
    for copy in away:
        copy.wait()


def body(queries, keys, values, tau, out_grad, key_blocks):
    anywhere = pl.BlockSpec(memory_space=pl.ANY)
    scalars = pl.BlockSpec(memory_space=pltpu.SMEM)
    shape = lambda a: (OWN, BLOCK, a.shape[2])
    chunk = (CHUNK, BLOCK, HD)
    blocked = [a.reshape(shape(a)) for a in (queries, keys, values, out_grad)]
    outs = pl.pallas_call(
        kernel,
        name="attention",
        out_shape=(
            jax.ShapeDtypeStruct(shape(queries), bf16),
            jax.ShapeDtypeStruct(shape(queries), bf16),
            jax.ShapeDtypeStruct(shape(keys), bf16),
            jax.ShapeDtypeStruct(shape(keys), bf16),
            jax.ShapeDtypeStruct((HEADS,), f32),
        ),
        in_specs=[scalars, scalars] + [anywhere] * 4,
        out_specs=(anywhere,) * 4 + (scalars,),
        scratch_shapes=[
            pltpu.VMEM((WINDOW, BLOCK, HD), bf16),
            pltpu.VMEM((WINDOW, BLOCK, HD), bf16),
            pltpu.VMEM((ROWS, BLOCK, WIDE), bf16),
            pltpu.VMEM((ROWS, BLOCK, WIDE), bf16),
            pltpu.VMEM((ROWS, LISTED, BLOCK, WIDE), f32),
            pltpu.VMEM((ROWS, LISTED, BLOCK, WIDE), bf16),
            pltpu.VMEM((ROWS, 8, WIDE), f32),
            pltpu.VMEM((ROWS, 8, WIDE), f32),
            pltpu.VMEM((WINDOW, BLOCK, HD), f32),
            pltpu.VMEM((WINDOW, BLOCK, HD), f32),
            pltpu.VMEM((ROWS, 2, BLOCK, WIDE), bf16),
            pltpu.VMEM((8 * PARTS,) + chunk, bf16),
            pltpu.VMEM((8 * PARTS,) + chunk, bf16),
            pltpu.VMEM((2 * PARTS,) + chunk, bf16),
            pltpu.VMEM((2 * PARTS,) + chunk, bf16),
            pltpu.VMEM((2, HALF, BLOCK, HD), bf16),
            pltpu.VMEM((8, WIDE), f32),
            pltpu.VMEM((NX, 8, BLOCK), f32),
            pltpu.VMEM((NY, NX, 8, BLOCK), f32),
            pltpu.VMEM((NZ * BATCH, NX, 8, BLOCK), f32),
            pltpu.SemaphoreType.DMA((8,)),
            pltpu.SemaphoreType.DMA((24 + 10 * PARTS,)),
            pltpu.SemaphoreType.DMA((24 + 10 * PARTS,)),
            pltpu.SemaphoreType.DMA((2 * ROWS,)),
            pltpu.SemaphoreType.DMA((2 * ROWS,)),
            pltpu.SemaphoreType.DMA((8 * PARTS,)),
            pltpu.SemaphoreType.DMA((8 * PARTS,)),
            pltpu.SemaphoreType.DMA((2 * PARTS,)),
            pltpu.SemaphoreType.DMA((2 * PARTS,)),
            pltpu.SemaphoreType.DMA((2 * NX * OWN,)),
            pltpu.SemaphoreType.DMA((2 * NX * OWN,)),
            pltpu.SemaphoreType.DMA((13,)),
            pltpu.SemaphoreType.DMA((13,)),
        ],
        compiler_params=pltpu.CompilerParams(
            collective_id=0, has_side_effects=True, vmem_limit_bytes=62 << 20
        ),
    )(key_blocks.transpose(2, 0, 1), tau, *blocked)
    outs = pl.pallas_call(
        copy_out,
        name="copy_out",
        out_shape=tuple(jax.ShapeDtypeStruct(o.shape, o.dtype) for o in outs),
        in_specs=[anywhere] * len(outs),
        out_specs=(anywhere,) * len(outs),
        scratch_shapes=[pltpu.VMEM(o.shape, o.dtype) for o in outs] + [pltpu.SemaphoreType.DMA((9,))] * 2,
    )(*outs)
    return tuple(o.reshape(a.shape) for o, a in zip(outs[:4], (queries, queries, keys, keys))) + (outs[4],)


def solution(mesh):
    sharded = P("batch", "ctx", None)
    return jax.shard_map(
        body,
        mesh=mesh,
        in_specs=(sharded, sharded, sharded, P(), sharded, P()),
        out_specs=(sharded, sharded, sharded, sharded, P()),
        check_vma=False,
    )
```

```python
import math

import jax
import jax.numpy as jnp
from jax import lax
from jax.experimental import pallas as pl
from jax.experimental.pallas import tpu as pltpu
from jax.sharding import PartitionSpec as P

HEADS = 16
GROUPS = 4
PER = HEADS // GROUPS
HD = 128
BLOCK = 128
BLOCKS = 64
WIDE = PER * HD
NY, NX, NZ = 4, 4, 2
OWN = 2
ROWS = NX * OWN
HALF = NX * OWN
PLANE = NZ * HALF
WINDOW = 3 * PLANE
PARTS = 2
CHUNK = HALF // PARTS
TOKENS = OWN * BLOCK
FIXED = (-1, 0, 1, 6, -6)
EITHER = ((2, 3), (-2, -3), (4, 9), (-4, -9), (8, 12), (-8, -12), (10, 15), (-10, -15))
LISTED = len(FIXED) + len(EITHER)
f32 = jnp.float32
bf16 = jnp.bfloat16
LOG2E = math.log2(math.e)
MESH = pl.DeviceIdType.MESH
BATCH = 4


def index_of(y, x, z):
    return lax.rem(y + NY, NY) * (NX * NZ) + lax.rem(x + NX, NX) * NZ + lax.rem(z, NZ)


def dot(a, b, ca, cb):
    return lax.dot_general(a, b, (((ca,), (cb,)), ((), ())), preferred_element_type=f32)


def kernel(
    key_blocks, tau_ref, queries, keys, values, grads,
    attended, query_grad, key_grad, value_grad, tau_out,
    kw, vw, q_all, g_all, s_all, ds_all, shift_all, dot_all, dk_acc, dv_acc, od,
    stage, arrived, z_stage, z_arrived, final, tau_acc, tau_x, tau_y, tau_z,
    here_sem, in_send, in_recv, od_send, od_recv, y_send, y_recv, z_send, z_recv, x_send, x_recv, tau_send, tau_recv,
):
    me = lax.axis_index("ctx")
    batch = lax.axis_index("batch")
    y, x, z = me // (NX * NZ), lax.rem(me // NZ, NX), lax.rem(me, NZ)

    def at(dy, dx, dz):
        return {"ctx": index_of(y + dy, x + dx, z + dz)}

    def far(dz, db):
        return {"ctx": index_of(y, x, z + dz), "batch": lax.rem(batch + db, BATCH)}

    def remote(src, dst, send, recv, device):
        return pltpu.make_async_remote_copy(
            src_ref=src, dst_ref=dst, send_sem=send, recv_sem=recv,
            device_id=device, device_id_type=MESH,
        )

    near_half = PLANE + z * HALF
    other_half = PLANE + (1 - z) * HALF

    def columns(array, n, place, width):
        return array.at[n, :, pl.ds(pl.multiple_of(place * width, width), width)]

    here_k, here_v, here_q, here_g = [
        [
            pltpu.make_async_copy(columns(array, n, x, width), place(0, n), here_sem.at[2 * i + n])
            for n in range(OWN)
        ]
        for i, (array, width, place) in enumerate(
            (
                (keys, HD, lambda d, n: kw.at[near_half + x * OWN + n]),
                (values, HD, lambda d, n: vw.at[near_half + x * OWN + n]),
                (queries, WIDE, lambda d, n: q_all.at[d * OWN + n]),
                (grads, WIDE, lambda d, n: g_all.at[d * OWN + n]),
            )
        )
    ]
    here = here_k + here_v + here_q + here_g
    for copy in here:
        copy.start()

    partners = [at(0, d, 0) for d in (1, 2, 3)] + [at(d, 0, 0) for d in (1, 2, 3)]
    partners += [far(dz, db) for dz in range(NZ) for db in range(BATCH) if dz or db]
    barrier = pltpu.get_barrier_semaphore()
    for device in partners:
        pl.semaphore_signal(barrier, inc=1, device_id=device, device_id_type=MESH)
    pl.semaphore_wait(barrier, len(partners))

    def along_x(array, width, place, first):
        out = []
        for d in (1, 2, 3):
            to = lax.rem(x + d, NX)
            for n in range(OWN):
                i = first + (d - 1) * OWN + n
                out.append(
                    remote(columns(array, n, to, width), place(d, n), in_send.at[i], in_recv.at[i], at(0, d, 0))
                )
        return out

    k_x = along_x(keys, HD, lambda d, n: kw.at[near_half + x * OWN + n], 0)
    v_x = along_x(values, HD, lambda d, n: vw.at[near_half + x * OWN + n], 6)
    q_x = along_x(queries, WIDE, lambda d, n: q_all.at[d * OWN + n], 12)
    g_x = along_x(grads, WIDE, lambda d, n: g_all.at[d * OWN + n], 18)

    def reached(half, part, side):
        low, high = part * CHUNK, (part + 1) * CHUNK
        if half == 1 and side == 0:
            low = max(low, 1)
        if half == 1 and side == 1:
            high = min(high, HALF - 1)
        return low, high - low

    def plane_sends(window, n):
        to_z, to_y = [], []
        for part in range(PARTS):
            span = window.at[pl.ds(near_half + part * CHUNK, CHUNK)]
            to_z.append(remote(span, span, in_send.at[n], in_recv.at[n], at(0, 0, 1)))
            n += 1
        for half, begin in ((1, near_half), (0, other_half)):
            to_y.append([])
            for part in range(PARTS):
                pair = []
                for side in range(2):
                    low, count = reached(half, part, side)
                    src = window.at[pl.ds(begin + low, count)]
                    dst = window.at[pl.ds(begin + low + (PLANE if side else -PLANE), count)]
                    pair.append(remote(src, dst, in_send.at[n], in_recv.at[n], at(3 if side else 1, 0, 0)))
                    n += 1
                to_y[-1].append(pair)
        return to_z, to_y[0], to_y[1]

    k_z, k_own, k_other = plane_sends(kw, 24)
    v_z, v_own, v_other = plane_sends(vw, 24 + 5 * PARTS)

    def start(copies):
        for copy in copies:
            copy.start()

    def received(copies):
        for copy in copies:
            copy.wait_recv()

    def wait(copies):
        for copy in copies:
            copy.wait()

    def flat(pairs):
        return [copy for pair in pairs for copy in pair]

    q_even, q_odd = q_x[0::OWN], q_x[1::OWN]
    g_even, g_odd = g_x[0::OWN], g_x[1::OWN]
    for copies in (k_x, v_x, q_even, q_odd, g_even, g_odd):
        start(copies)
    dk_acc[...] = jnp.zeros_like(dk_acc)
    dv_acc[...] = jnp.zeros_like(dv_acc)
    for window in (kw, vw):
        for end in (z * HALF, 2 * PLANE + z * HALF + HALF - 1):
            window[end] = jnp.zeros((BLOCK, HD), bf16)
    scale = jnp.concatenate(
        [jnp.full((1, BLOCK), tau_ref[x * PER + h] / math.sqrt(HD), f32) for h in range(PER)], 1
    )
    scale_two = scale * LOG2E
    log_scale = jnp.log(scale) * LOG2E
    wait(here_k)
    received(k_x)
    start(k_z)
    start(flat(k_own))
    wait(here_v)
    received(v_x)
    start(v_z)
    for part in range(PARTS):
        received(k_z[part : part + 1])
        start(k_other[part])
    start(flat(v_own))
    wait(here_q)
    received(q_even)
    received(flat(k_own))
    for part in range(PARTS):
        received(v_z[part : part + 1])
        start(v_other[part])
    received(flat(k_other))

    def row_at(step):
        return lax.rem(ROWS + ROWS // 2 - OWN * lax.rem(step, NX), ROWS) + step // NX

    def row_place(r):
        return lax.rem(x - r // OWN + NX, NX) * (NZ * OWN) + z * OWN + lax.rem(r, OWN)

    def slot_of(linear):
        rest = lax.rem(linear, PLANE)
        return (linear // PLANE) * PLANE + lax.rem(rest // OWN, NZ) * HALF + (rest // (NZ * OWN)) * OWN + lax.rem(rest, OWN)

    def is_two(r):
        a = y * PLANE + row_place(r)
        sought = lax.rem(a + 2, BLOCKS)
        hit = 0
        for k in range(LISTED):
            hit = jnp.where(key_blocks[k, x, a] == sought, 1, hit)
        return hit

    def slots(r):
        linear = PLANE + row_place(r)
        fixed = [slot_of(linear + o) for o in FIXED]
        either = [(slot_of(linear + two), slot_of(linear + three)) for two, three in EITHER]
        two = is_two(r)
        picks = fixed + [jnp.where(two == 1, p, q) for p, q in either]
        weight = two.astype(f32)

        def add(acc, k, part):
            if k < len(FIXED):
                acc[fixed[k]] += part
            else:
                p, q = either[k - len(FIXED)]
                acc[p] += part * weight
                acc[q] += part * (1.0 - weight)

        return picks, add

    def heads_of(array, r):
        return jnp.concatenate([array[r, :, h * HD : (h + 1) * HD] for h in range(PER)], 0)

    def folded(array, join):
        rows = BLOCK
        while rows > 8:
            rows //= 2
            array = join(array[:rows], array[rows:])
        return array

    def scores(r):
        q = heads_of(q_all, r)
        picks, _ = slots(r)
        high = None
        for k in range(LISTED):
            s = dot(kw[picks[k]], q, 1, 1) * scale_two
            s_all[r, k] = s
            top = folded(s, jnp.maximum)
            high = top if high is None else jnp.maximum(high, top)
        high = high.max(0, keepdims=True)
        total = jnp.zeros((8, WIDE), f32)
        for k in range(LISTED):
            total = total + folded(jnp.exp2(s_all[r, k] - high), jnp.add)
        log_total = jnp.log(total.sum(0, keepdims=True)) * LOG2E
        shift_all[r] = jnp.broadcast_to(high + log_total, (8, WIDE))

    def even_scores(i, _):
        scores(i * OWN)
        return 0

    def odd_scores(i, _):
        scores(i * OWN + 1)
        return 0

    lax.fori_loop(0, NX, even_scores, 0)
    received(q_odd)
    lax.fori_loop(0, NX, odd_scores, 0)
    wait(here_g)
    received(g_even)
    received(flat(v_own))
    received(flat(v_other))

    def back(r, which, out, local):
        d, half = r // OWN, lax.rem(r, OWN)
        dst = columns(out, half, x, WIDE)
        n = which * ROWS + r
        if local:
            return pltpu.make_async_copy(od.at[r, which], dst, od_recv.at[n])
        return remote(od.at[r, which], dst, od_send.at[n], od_recv.at[n], at(0, NX - d, 0))

    def put_back(r, which, result):
        for h in range(PER):
            od[r, which, :, h * HD : (h + 1) * HD] = result[h * BLOCK : (h + 1) * BLOCK].astype(bf16)

    def send_back(r, which, out):
        @pl.when(r < OWN)
        def _():
            back(r, which, out, True).start()

        @pl.when(r >= OWN)
        def _():
            back(r, which, out, False).start()

    def output(r):
        g = heads_of(g_all, r)
        picks, add = slots(r)
        shift = shift_all[r, 0:1]
        o = None
        for k in range(LISTED):
            p = jnp.exp2(s_all[r, k] - shift).astype(bf16)
            add(dv_acc, k, dot(p, g, 1, 0))
            part = dot(p, vw[picks[k]], 0, 0)
            o = part if o is None else o + part
        put_back(r, 0, o)
        row_dot = (g.astype(f32) * o).sum(-1, keepdims=True)
        dot_all[r] = jnp.broadcast_to(row_dot, (WIDE, HD)).T[0:8]

    def outputs(i, _):
        @pl.when(i == NX // 2)
        def _():
            received(g_odd)

        pair = [row_at(2 * i), row_at(2 * i + 1)]
        for r in pair:
            output(r)
        for r in pair:
            send_back(r, 0, attended)
        return 0

    lax.fori_loop(0, ROWS // 2, outputs, 0)

    accs = (dv_acc, dk_acc)
    outs = (value_grad, key_grad)

    def y_copy(kv, half, part, side):
        n = ((kv * 2 + half) * PARTS + part) * 2 + side
        span = pl.ds(0, reached(half, part, side)[1])
        return remote(stage.at[n, span], arrived.at[n, span], y_send.at[n], y_recv.at[n], at(3 if side == 0 else 1, 0, 0))

    def z_copy(kv, part):
        n = kv * PARTS + part
        return remote(z_stage.at[n], z_arrived.at[n], z_send.at[n], z_recv.at[n], at(0, 0, 1))

    def x_copy(kv, to, m, local):
        src = final.at[kv, to * OWN + m]
        dst = columns(outs[kv], m, x, HD)
        n = (kv * NX + x) * OWN + m
        if local:
            return pltpu.make_async_copy(src, dst, x_recv.at[n])
        return remote(src, dst, x_send.at[(kv * NX + to) * OWN + m], x_recv.at[n], {"ctx": index_of(y, to, z)})

    def x_arrival(kv, d, m):
        dst = columns(outs[kv], m, lax.rem(x + d, NX), HD)
        n = (kv * NX + lax.rem(x + d, NX)) * OWN + m
        return remote(final.at[kv, m], dst, x_send.at[n], x_recv.at[n], at(0, d, 0))

    def both(kv, half, part):
        return [y_copy(kv, half, part, side) for side in range(2)]

    def to_y(kv):
        for half in range(2):
            for part in range(PARTS):
                for side in range(2):
                    low, count = reached(half, part, side)
                    begin = side * 2 * PLANE + (1 - z if half == 0 else z) * HALF + low
                    n = ((kv * 2 + half) * PARTS + part) * 2 + side
                    stage[n, :count] = accs[kv][pl.ds(begin, count)].astype(bf16)
                    y_copy(kv, half, part, side).start()

    def collected(kv, half, part, begin):
        received(both(kv, half, part))
        for side in range(2):
            low, count = reached(half, part, side)
            n = ((kv * 2 + half) * PARTS + part) * 2 + side
            accs[kv][pl.ds(begin + low, count)] += arrived[n, :count].astype(f32)
        return accs[kv][pl.ds(begin + part * CHUNK, CHUNK)]

    def to_z(kv, part):
        z_stage[kv * PARTS + part] = collected(kv, 0, part, other_half).astype(bf16)
        z_copy(kv, part).start()

    def to_x(kv, part):
        summed = collected(kv, 1, part, near_half)
        z_copy(kv, part).wait_recv()
        summed = summed + z_arrived[kv * PARTS + part].astype(f32)
        final[kv, part * CHUNK : (part + 1) * CHUNK] = summed.astype(bf16)
        for i in range(CHUNK // OWN):
            to = part * (CHUNK // OWN) + i

            @pl.when(to == x)
            def _():
                for m in range(OWN):
                    x_copy(kv, to, m, True).start()

            @pl.when(to != x)
            def _():
                for m in range(OWN):
                    x_copy(kv, to, m, False).start()

    to_y(0)
    tau_acc[...] = jnp.zeros_like(tau_acc)

    def score_grads(step, _):
        for part in range(PARTS):

            @pl.when(step == 3 + part)
            def _(part=part):
                to_z(0, part)

            @pl.when(step == ROWS - PARTS + part)
            def _(part=part):
                to_x(0, part)

        r = step
        q = heads_of(q_all, r)
        g = heads_of(g_all, r)
        picks, add = slots(r)
        row_dot = dot_all[r, 0:1]
        shift = shift_all[r, 0:1] - log_scale
        tau = jnp.zeros((8, WIDE), f32)
        for k in range(LISTED):
            s = s_all[r, k]
            t = jnp.exp2(s - shift) * (dot(vw[picks[k]], g, 1, 1) - row_dot)
            tau = tau + folded(t * s, jnp.add)
            ds_all[r, k] = t.astype(bf16)
        for k in range(LISTED):
            add(dk_acc, k, dot(ds_all[r, k], q, 1, 0))
        tau_acc[...] += tau / (scale * scale_two)
        return 0

    lax.fori_loop(0, ROWS, score_grads, 0)
    to_y(1)

    parts = jnp.concatenate([tau_acc[:, h * BLOCK : (h + 1) * BLOCK].sum(0, keepdims=True) for h in range(PER)], 0)
    tau_x[x] = jnp.concatenate([parts, jnp.zeros_like(parts)], 0)
    tau_first = [remote(tau_x.at[x], tau_x.at[x], tau_send.at[d - 1], tau_recv.at[d - 1], at(0, d, 0)) for d in (1, 2, 3)]
    start(tau_first)

    def query_grads(step, _):
        r = row_at(step)
        picks, _ = slots(r)
        dq = None
        for k in range(LISTED):
            part = dot(ds_all[r, k], kw[picks[k]], 0, 0)
            dq = part if dq is None else dq + part
        put_back(r, 1, dq)
        send_back(r, 1, query_grad)
        return 0

    lax.fori_loop(0, ROWS // 2, query_grads, 0)
    received(tau_first)
    tau_y[y] = tau_x[...]
    tau_second = [remote(tau_y.at[y], tau_y.at[y], tau_send.at[d + 2], tau_recv.at[d + 2], at(d, 0, 0)) for d in (1, 2, 3)]
    start(tau_second)
    to_z(1, 0)
    lax.fori_loop(ROWS // 2, ROWS, query_grads, 0)
    for part in range(1, PARTS):
        to_z(1, part)
    received(tau_second)
    spot = z * BATCH + batch
    tau_z[spot] = tau_y[0] + tau_y[1] + tau_y[2] + tau_y[3]
    tau_third = []
    for dz in range(NZ):
        for db in range(BATCH):
            if dz or db:
                n = 6 + len(tau_third)
                tau_third.append(remote(tau_z.at[spot], tau_z.at[spot], tau_send.at[n], tau_recv.at[n], far(dz, db)))
    start(tau_third)
    for part in range(PARTS):
        to_x(1, part)
    received(tau_third)
    whole = tau_z[0]
    for n in range(1, NZ * BATCH):
        whole = whole + tau_z[n]
    norm = math.sqrt(HD) * math.sqrt(BATCH * NY * NX * NZ * TOKENS)
    for n in range(NX):
        for h in range(PER):
            tau_out[n * PER + h] = jnp.sum(whole[n, h : h + 1, :]) / norm

    for which, out in enumerate((attended, query_grad)):
        for r in range(ROWS):
            back(r, which, out, r < OWN).wait()
    for kv in range(2):
        for m in range(OWN):
            x_copy(kv, x, m, True).wait()
            for d in (1, 2, 3):
                x_arrival(kv, d, m).wait_recv()
                x_copy(kv, lax.rem(x + d, NX), m, False).wait_send()
        for part in range(PARTS):
            z_copy(kv, part).wait_send()
            for half in range(2):
                for copy in both(kv, half, part):
                    copy.wait_send()
    for copy in k_x + v_x + q_x + g_x + k_z + v_z + flat(k_own + k_other + v_own + v_other) + tau_first + tau_second + tau_third:
        copy.wait_send()


def copy_out(*refs):
    n = (len(refs) - 2) // 3
    sources, results, held = refs[:n], refs[n : 2 * n], refs[2 * n : 3 * n]
    in_sem, out_sem = refs[3 * n :]
    pieces = [(i, m) for i in range(n) for m in range(OWN if i < n - 1 else 1)]

    def piece(ref, i, m):
        return ref.at[m] if i < n - 1 else ref

    into = [pltpu.make_async_copy(piece(sources[i], i, m), piece(held[i], i, m), in_sem.at[j]) for j, (i, m) in enumerate(pieces)]
    away = [pltpu.make_async_copy(piece(held[i], i, m), piece(results[i], i, m), out_sem.at[j]) for j, (i, m) in enumerate(pieces)]
    for copy in into:
        copy.start()
    for first, second in zip(into, away):
        first.wait()
        second.start()
    for copy in away:
        copy.wait()


def body(queries, keys, values, tau, out_grad, key_blocks):
    anywhere = pl.BlockSpec(memory_space=pl.ANY)
    scalars = pl.BlockSpec(memory_space=pltpu.SMEM)
    shape = lambda a: (OWN, BLOCK, a.shape[2])
    chunk = (CHUNK, BLOCK, HD)
    blocked = [a.reshape(shape(a)) for a in (queries, keys, values, out_grad)]
    outs = pl.pallas_call(
        kernel,
        name="attention",
        out_shape=(
            jax.ShapeDtypeStruct(shape(queries), bf16),
            jax.ShapeDtypeStruct(shape(queries), bf16),
            jax.ShapeDtypeStruct(shape(keys), bf16),
            jax.ShapeDtypeStruct(shape(keys), bf16),
            jax.ShapeDtypeStruct((HEADS,), f32),
        ),
        in_specs=[scalars, scalars] + [anywhere] * 4,
        out_specs=(anywhere,) * 4 + (scalars,),
        scratch_shapes=[
            pltpu.VMEM((WINDOW, BLOCK, HD), bf16),
            pltpu.VMEM((WINDOW, BLOCK, HD), bf16),
            pltpu.VMEM((ROWS, BLOCK, WIDE), bf16),
            pltpu.VMEM((ROWS, BLOCK, WIDE), bf16),
            pltpu.VMEM((ROWS, LISTED, BLOCK, WIDE), f32),
            pltpu.VMEM((ROWS, LISTED, BLOCK, WIDE), bf16),
            pltpu.VMEM((ROWS, 8, WIDE), f32),
            pltpu.VMEM((ROWS, 8, WIDE), f32),
            pltpu.VMEM((WINDOW, BLOCK, HD), f32),
            pltpu.VMEM((WINDOW, BLOCK, HD), f32),
            pltpu.VMEM((ROWS, 2, BLOCK, WIDE), bf16),
            pltpu.VMEM((8 * PARTS,) + chunk, bf16),
            pltpu.VMEM((8 * PARTS,) + chunk, bf16),
            pltpu.VMEM((2 * PARTS,) + chunk, bf16),
            pltpu.VMEM((2 * PARTS,) + chunk, bf16),
            pltpu.VMEM((2, HALF, BLOCK, HD), bf16),
            pltpu.VMEM((8, WIDE), f32),
            pltpu.VMEM((NX, 8, BLOCK), f32),
            pltpu.VMEM((NY, NX, 8, BLOCK), f32),
            pltpu.VMEM((NZ * BATCH, NX, 8, BLOCK), f32),
            pltpu.SemaphoreType.DMA((8,)),
            pltpu.SemaphoreType.DMA((24 + 10 * PARTS,)),
            pltpu.SemaphoreType.DMA((24 + 10 * PARTS,)),
            pltpu.SemaphoreType.DMA((2 * ROWS,)),
            pltpu.SemaphoreType.DMA((2 * ROWS,)),
            pltpu.SemaphoreType.DMA((8 * PARTS,)),
            pltpu.SemaphoreType.DMA((8 * PARTS,)),
            pltpu.SemaphoreType.DMA((2 * PARTS,)),
            pltpu.SemaphoreType.DMA((2 * PARTS,)),
            pltpu.SemaphoreType.DMA((2 * NX * OWN,)),
            pltpu.SemaphoreType.DMA((2 * NX * OWN,)),
            pltpu.SemaphoreType.DMA((13,)),
            pltpu.SemaphoreType.DMA((13,)),
        ],
        compiler_params=pltpu.CompilerParams(
            collective_id=0, has_side_effects=True, vmem_limit_bytes=62 << 20
        ),
    )(key_blocks.transpose(2, 0, 1), tau, *blocked)
    outs = pl.pallas_call(
        copy_out,
        name="copy_out",
        out_shape=tuple(jax.ShapeDtypeStruct(o.shape, o.dtype) for o in outs),
        in_specs=[anywhere] * len(outs),
        out_specs=(anywhere,) * len(outs),
        scratch_shapes=[pltpu.VMEM(o.shape, o.dtype) for o in outs] + [pltpu.SemaphoreType.DMA((9,))] * 2,
    )(*outs)
    return tuple(o.reshape(a.shape) for o, a in zip(outs[:4], (queries, queries, keys, keys))) + (outs[4],)


def solution(mesh):
    sharded = P("batch", "ctx", None)
    return jax.shard_map(
        body,
        mesh=mesh,
        in_specs=(sharded, sharded, sharded, P(), sharded, P()),
        out_specs=(sharded, sharded, sharded, sharded, P()),
        check_vma=False,
    )
```

```python
import math

import jax
import jax.numpy as jnp
from jax import lax
from jax.experimental import pallas as pl
from jax.experimental.pallas import tpu as pltpu
from jax.sharding import PartitionSpec as P

HEADS = 16
GROUPS = 4
PER = HEADS // GROUPS
HD = 128
BLOCK = 128
BLOCKS = 64
WIDE = PER * HD
NY, NX, NZ = 4, 4, 2
OWN = 2
ROWS = NX * OWN
HALF = NX * OWN
PLANE = NZ * HALF
WINDOW = 3 * PLANE
PARTS = 2
CHUNK = HALF // PARTS
REACHED = {
    (0, 0): (((0, 1), (2, 2)), ((4, 4),)),
    (0, 1): (((0, 4),), ((4, 2), (7, 1))),
    (1, 0): (((1, 3),), ((4, 4),)),
    (1, 1): (((0, 4),), ((4, 3),)),
}
PIECES = [
    (half, part, side, low, count)
    for half in range(2)
    for part in range(PARTS)
    for side in range(2)
    for low, count in REACHED[half, side][part]
]


def pieces(half, part):
    return [(n, p[2], p[3], p[4]) for n, p in enumerate(PIECES) if p[:2] == (half, part)]

TOKENS = OWN * BLOCK
FIXED = (-1, 0, 1, 6, -6)
EITHER = ((2, 3), (-2, -3), (4, 9), (-4, -9), (8, 12), (-8, -12), (10, 15), (-10, -15))
LISTED = len(FIXED) + len(EITHER)
f32 = jnp.float32
bf16 = jnp.bfloat16
LOG2E = math.log2(math.e)
MESH = pl.DeviceIdType.MESH
BATCH = 4


def index_of(y, x, z):
    return lax.rem(y + NY, NY) * (NX * NZ) + lax.rem(x + NX, NX) * NZ + lax.rem(z, NZ)


def dot(a, b, ca, cb):
    return lax.dot_general(a, b, (((ca,), (cb,)), ((), ())), preferred_element_type=f32)


def kernel(
    key_blocks, tau_ref, queries, keys, values, grads,
    attended, query_grad, key_grad, value_grad, tau_out,
    kw, vw, q_all, g_all, s_all, ds_all, shift_all, dot_all, dk_acc, dv_acc, od,
    stage, arrived, z_stage, z_arrived, final, tau_acc, tau_x, tau_y, tau_z,
    here_sem, in_send, in_recv, od_send, od_recv, y_send, y_recv, z_send, z_recv, x_send, x_recv, tau_send, tau_recv,
):
    me = lax.axis_index("ctx")
    batch = lax.axis_index("batch")
    y, x, z = me // (NX * NZ), lax.rem(me // NZ, NX), lax.rem(me, NZ)

    def at(dy, dx, dz):
        return {"ctx": index_of(y + dy, x + dx, z + dz)}

    def far(dz, db):
        return {"ctx": index_of(y, x, z + dz), "batch": lax.rem(batch + db, BATCH)}

    def remote(src, dst, send, recv, device):
        return pltpu.make_async_remote_copy(
            src_ref=src, dst_ref=dst, send_sem=send, recv_sem=recv,
            device_id=device, device_id_type=MESH,
        )

    near_half = PLANE + z * HALF
    other_half = PLANE + (1 - z) * HALF

    def columns(array, n, place, width):
        return array.at[n, :, pl.ds(pl.multiple_of(place * width, width), width)]

    here_k, here_v, here_q, here_g = [
        [
            pltpu.make_async_copy(columns(array, n, x, width), place(0, n), here_sem.at[2 * i + n])
            for n in range(OWN)
        ]
        for i, (array, width, place) in enumerate(
            (
                (keys, HD, lambda d, n: kw.at[near_half + x * OWN + n]),
                (values, HD, lambda d, n: vw.at[near_half + x * OWN + n]),
                (queries, WIDE, lambda d, n: q_all.at[d * OWN + n]),
                (grads, WIDE, lambda d, n: g_all.at[d * OWN + n]),
            )
        )
    ]
    here = here_k + here_v + here_q + here_g
    for copy in here:
        copy.start()

    partners = [at(0, d, 0) for d in (1, 2, 3)] + [at(d, 0, 0) for d in (1, 2, 3)]
    partners += [far(dz, db) for dz in range(NZ) for db in range(BATCH) if dz or db]
    barrier = pltpu.get_barrier_semaphore()
    for device in partners:
        pl.semaphore_signal(barrier, inc=1, device_id=device, device_id_type=MESH)
    pl.semaphore_wait(barrier, len(partners))

    def along_x(array, width, place, first):
        out = []
        for d in (1, 2, 3):
            to = lax.rem(x + d, NX)
            for n in range(OWN):
                i = first + (d - 1) * OWN + n
                out.append(
                    remote(columns(array, n, to, width), place(d, n), in_send.at[i], in_recv.at[i], at(0, d, 0))
                )
        return out

    k_x = along_x(keys, HD, lambda d, n: kw.at[near_half + x * OWN + n], 0)
    v_x = along_x(values, HD, lambda d, n: vw.at[near_half + x * OWN + n], 6)
    q_x = along_x(queries, WIDE, lambda d, n: q_all.at[d * OWN + n], 12)
    g_x = along_x(grads, WIDE, lambda d, n: g_all.at[d * OWN + n], 18)

    def plane_sends(window, n):
        to_z, to_y = [], []
        for part in range(PARTS):
            span = window.at[pl.ds(near_half + part * CHUNK, CHUNK)]
            to_z.append(remote(span, span, in_send.at[n], in_recv.at[n], at(0, 0, 1)))
            n += 1
        for half, begin in ((1, near_half), (0, other_half)):
            to_y.append([])
            for part in range(PARTS):
                pair = []
                for _, side, low, count in pieces(half, part):
                    src = window.at[pl.ds(begin + low, count)]
                    dst = window.at[pl.ds(begin + low + (PLANE if side else -PLANE), count)]
                    pair.append(remote(src, dst, in_send.at[n], in_recv.at[n], at(3 if side else 1, 0, 0)))
                    n += 1
                to_y[-1].append(pair)
        return to_z, to_y[0], to_y[1]

    k_z, k_own, k_other = plane_sends(kw, 24)
    v_z, v_own, v_other = plane_sends(vw, 24 + PARTS + len(PIECES))

    def start(copies):
        for copy in copies:
            copy.start()

    def received(copies):
        for copy in copies:
            copy.wait_recv()

    def wait(copies):
        for copy in copies:
            copy.wait()

    def flat(pairs):
        return [copy for pair in pairs for copy in pair]

    q_even, q_odd = q_x[0::OWN], q_x[1::OWN]
    g_even, g_odd = g_x[0::OWN], g_x[1::OWN]
    for copies in (k_x, v_x, q_even, q_odd, g_even, g_odd):
        start(copies)
    dk_acc[...] = jnp.zeros_like(dk_acc)
    dv_acc[...] = jnp.zeros_like(dv_acc)
    for window in (kw, vw):
        for end in (
            z * HALF, 2 * PLANE + z * HALF + HALF - 1,
            (1 - z) * HALF + 1, 2 * PLANE + (1 - z) * HALF + 6,
        ):
            window[end] = jnp.zeros((BLOCK, HD), bf16)
    scale = jnp.concatenate(
        [jnp.full((1, BLOCK), tau_ref[x * PER + h] / math.sqrt(HD), f32) for h in range(PER)], 1
    )
    scale_two = scale * LOG2E
    log_scale = jnp.log(scale) * LOG2E
    wait(here_k)
    received(k_x)
    start(k_z)
    start(flat(k_own))
    wait(here_v)
    received(v_x)
    start(v_z)
    for part in range(PARTS):
        received(k_z[part : part + 1])
        start(k_other[part])
    start(flat(v_own))
    wait(here_q)
    received(q_even)
    received(flat(k_own))
    for part in range(PARTS):
        received(v_z[part : part + 1])
        start(v_other[part])
    received(flat(k_other))

    def row_at(step):
        return lax.rem(ROWS + ROWS // 2 - OWN * lax.rem(step, NX), ROWS) + step // NX

    def row_place(r):
        return lax.rem(x - r // OWN + NX, NX) * (NZ * OWN) + z * OWN + lax.rem(r, OWN)

    def slot_of(linear):
        rest = lax.rem(linear, PLANE)
        return (linear // PLANE) * PLANE + lax.rem(rest // OWN, NZ) * HALF + (rest // (NZ * OWN)) * OWN + lax.rem(rest, OWN)

    def is_two(r):
        a = y * PLANE + row_place(r)
        sought = lax.rem(a + 2, BLOCKS)
        hit = 0
        for k in range(LISTED):
            hit = jnp.where(key_blocks[k, x, a] == sought, 1, hit)
        return hit

    def slots(r):
        linear = PLANE + row_place(r)
        fixed = [slot_of(linear + o) for o in FIXED]
        either = [(slot_of(linear + two), slot_of(linear + three)) for two, three in EITHER]
        two = is_two(r)
        picks = fixed + [jnp.where(two == 1, p, q) for p, q in either]
        weight = two.astype(f32)

        def add(acc, k, part):
            if k < len(FIXED):
                acc[fixed[k]] += part
            else:
                p, q = either[k - len(FIXED)]
                acc[p] += part * weight
                acc[q] += part * (1.0 - weight)

        return picks, add

    def heads_of(array, r):
        return jnp.concatenate([array[r, :, h * HD : (h + 1) * HD] for h in range(PER)], 0)

    def folded(array, join):
        rows = BLOCK
        while rows > 8:
            rows //= 2
            array = join(array[:rows], array[rows:])
        return array

    def scores(r):
        q = heads_of(q_all, r)
        picks, _ = slots(r)
        high = None
        for k in range(LISTED):
            s = dot(kw[picks[k]], q, 1, 1) * scale_two
            s_all[r, k] = s
            top = folded(s, jnp.maximum)
            high = top if high is None else jnp.maximum(high, top)
        high = high.max(0, keepdims=True)
        total = jnp.zeros((8, WIDE), f32)
        for k in range(LISTED):
            total = total + folded(jnp.exp2(s_all[r, k] - high), jnp.add)
        log_total = jnp.log(total.sum(0, keepdims=True)) * LOG2E
        shift_all[r] = jnp.broadcast_to(high + log_total, (8, WIDE))

    def even_scores(i, _):
        scores(i * OWN)
        return 0

    def odd_scores(i, _):
        scores(i * OWN + 1)
        return 0

    lax.fori_loop(0, NX, even_scores, 0)
    received(q_odd)
    lax.fori_loop(0, NX, odd_scores, 0)
    wait(here_g)
    received(g_even)
    received(flat(v_own))
    received(flat(v_other))

    def back(r, which, out, local):
        d, half = r // OWN, lax.rem(r, OWN)
        dst = columns(out, half, x, WIDE)
        n = which * ROWS + r
        if local:
            return pltpu.make_async_copy(od.at[r, which], dst, od_recv.at[n])
        return remote(od.at[r, which], dst, od_send.at[n], od_recv.at[n], at(0, NX - d, 0))

    def put_back(r, which, result):
        for h in range(PER):
            od[r, which, :, h * HD : (h + 1) * HD] = result[h * BLOCK : (h + 1) * BLOCK].astype(bf16)

    def send_back(r, which, out):
        @pl.when(r < OWN)
        def _():
            back(r, which, out, True).start()

        @pl.when(r >= OWN)
        def _():
            back(r, which, out, False).start()

    def output(r):
        g = heads_of(g_all, r)
        picks, add = slots(r)
        shift = shift_all[r, 0:1]
        o = None
        for k in range(LISTED):
            p = jnp.exp2(s_all[r, k] - shift).astype(bf16)
            add(dv_acc, k, dot(p, g, 1, 0))
            part = dot(p, vw[picks[k]], 0, 0)
            o = part if o is None else o + part
        put_back(r, 0, o)
        row_dot = (g.astype(f32) * o).sum(-1, keepdims=True)
        dot_all[r] = jnp.broadcast_to(row_dot, (WIDE, HD)).T[0:8]

    def outputs(i, _):
        @pl.when(i == NX // 2)
        def _():
            received(g_odd)

        pair = [row_at(2 * i), row_at(2 * i + 1)]
        for r in pair:
            output(r)
        for r in pair:
            send_back(r, 0, attended)
        return 0

    lax.fori_loop(0, ROWS // 2, outputs, 0)

    accs = (dv_acc, dk_acc)
    outs = (value_grad, key_grad)

    def held(kv, piece):
        half, part, side, low, _ = PIECES[piece]
        return ((kv * 2 + half) * PARTS + part) * 2 + side, low - part * CHUNK

    def y_copy(kv, piece, side, count):
        n = kv * len(PIECES) + piece
        slot, first = held(kv, piece)
        span = pl.ds(first, count)
        return remote(stage.at[slot, span], arrived.at[slot, span], y_send.at[n], y_recv.at[n], at(3 if side == 0 else 1, 0, 0))

    def z_copy(kv, part):
        n = kv * PARTS + part
        return remote(z_stage.at[n], z_arrived.at[n], z_send.at[n], z_recv.at[n], at(0, 0, 1))

    def x_copy(kv, to, m, local):
        src = final.at[kv, to * OWN + m]
        dst = columns(outs[kv], m, x, HD)
        n = (kv * NX + x) * OWN + m
        if local:
            return pltpu.make_async_copy(src, dst, x_recv.at[n])
        return remote(src, dst, x_send.at[(kv * NX + to) * OWN + m], x_recv.at[n], {"ctx": index_of(y, to, z)})

    def x_arrival(kv, d, m):
        dst = columns(outs[kv], m, lax.rem(x + d, NX), HD)
        n = (kv * NX + lax.rem(x + d, NX)) * OWN + m
        return remote(final.at[kv, m], dst, x_send.at[n], x_recv.at[n], at(0, d, 0))

    def both(kv, half, part):
        return [y_copy(kv, n, side, count) for n, side, _, count in pieces(half, part)]

    def to_y(kv):
        for n, (half, part, side, low, count) in enumerate(PIECES):
            begin = side * 2 * PLANE + (1 - z if half == 0 else z) * HALF + low
            slot, first = held(kv, n)
            stage[slot, first : first + count] = accs[kv][pl.ds(begin, count)].astype(bf16)
            y_copy(kv, n, side, count).start()

    def collected(kv, half, part, begin):
        received(both(kv, half, part))
        for n, side, low, count in pieces(half, part):
            slot, first = held(kv, n)
            accs[kv][pl.ds(begin + low, count)] += arrived[slot, first : first + count].astype(f32)
        return accs[kv][pl.ds(begin + part * CHUNK, CHUNK)]

    def to_z(kv, part):
        z_stage[kv * PARTS + part] = collected(kv, 0, part, other_half).astype(bf16)
        z_copy(kv, part).start()

    def to_x(kv, part):
        summed = collected(kv, 1, part, near_half)
        z_copy(kv, part).wait_recv()
        summed = summed + z_arrived[kv * PARTS + part].astype(f32)
        final[kv, part * CHUNK : (part + 1) * CHUNK] = summed.astype(bf16)
        for i in range(CHUNK // OWN):
            to = part * (CHUNK // OWN) + i

            @pl.when(to == x)
            def _():
                for m in range(OWN):
                    x_copy(kv, to, m, True).start()

            @pl.when(to != x)
            def _():
                for m in range(OWN):
                    x_copy(kv, to, m, False).start()

    to_y(0)
    tau_acc[...] = jnp.zeros_like(tau_acc)

    def score_grads(step, _):
        for part in range(PARTS):

            @pl.when(step == 3 + part)
            def _(part=part):
                to_z(0, part)

            @pl.when(step == ROWS - PARTS + part)
            def _(part=part):
                to_x(0, part)

        r = step
        q = heads_of(q_all, r)
        g = heads_of(g_all, r)
        picks, add = slots(r)
        row_dot = dot_all[r, 0:1]
        shift = shift_all[r, 0:1] - log_scale
        tau = jnp.zeros((8, WIDE), f32)
        for k in range(LISTED):
            s = s_all[r, k]
            t = jnp.exp2(s - shift) * (dot(vw[picks[k]], g, 1, 1) - row_dot)
            tau = tau + folded(t * s, jnp.add)
            ds_all[r, k] = t.astype(bf16)
        for k in range(LISTED):
            add(dk_acc, k, dot(ds_all[r, k], q, 1, 0))
        tau_acc[...] += tau / (scale * scale_two)
        return 0

    lax.fori_loop(0, ROWS, score_grads, 0)
    to_y(1)

    parts = jnp.concatenate([tau_acc[:, h * BLOCK : (h + 1) * BLOCK].sum(0, keepdims=True) for h in range(PER)], 0)
    tau_x[x] = jnp.concatenate([parts, jnp.zeros_like(parts)], 0)
    tau_first = [remote(tau_x.at[x], tau_x.at[x], tau_send.at[d - 1], tau_recv.at[d - 1], at(0, d, 0)) for d in (1, 2, 3)]
    start(tau_first)

    def query_grads(i, _):
        pair = [row_at(2 * i), row_at(2 * i + 1)]
        for r in pair:
            picks, _ = slots(r)
            dq = None
            for k in range(LISTED):
                part = dot(ds_all[r, k], kw[picks[k]], 0, 0)
                dq = part if dq is None else dq + part
            put_back(r, 1, dq)
        for r in pair:
            send_back(r, 1, query_grad)
        return 0

    lax.fori_loop(0, ROWS // 4, query_grads, 0)
    received(tau_first)
    tau_y[y] = tau_x[...]
    tau_second = [remote(tau_y.at[y], tau_y.at[y], tau_send.at[d + 2], tau_recv.at[d + 2], at(d, 0, 0)) for d in (1, 2, 3)]
    start(tau_second)
    to_z(1, 0)
    lax.fori_loop(ROWS // 4, ROWS // 2, query_grads, 0)
    for part in range(1, PARTS):
        to_z(1, part)
    received(tau_second)
    spot = z * BATCH + batch
    tau_z[spot] = tau_y[0] + tau_y[1] + tau_y[2] + tau_y[3]
    tau_third = []
    for dz in range(NZ):
        for db in range(BATCH):
            if dz or db:
                n = 6 + len(tau_third)
                tau_third.append(remote(tau_z.at[spot], tau_z.at[spot], tau_send.at[n], tau_recv.at[n], far(dz, db)))
    start(tau_third)
    for part in range(PARTS):
        to_x(1, part)
    received(tau_third)
    whole = tau_z[0]
    for n in range(1, NZ * BATCH):
        whole = whole + tau_z[n]
    norm = math.sqrt(HD) * math.sqrt(BATCH * NY * NX * NZ * TOKENS)
    for n in range(NX):
        for h in range(PER):
            tau_out[n * PER + h] = jnp.sum(whole[n, h : h + 1, :]) / norm

    for which, out in enumerate((attended, query_grad)):
        for r in range(ROWS):
            back(r, which, out, r < OWN).wait()
    for kv in range(2):
        for m in range(OWN):
            x_copy(kv, x, m, True).wait()
            for d in (1, 2, 3):
                x_arrival(kv, d, m).wait_recv()
                x_copy(kv, lax.rem(x + d, NX), m, False).wait_send()
        for part in range(PARTS):
            z_copy(kv, part).wait_send()
            for half in range(2):
                for copy in both(kv, half, part):
                    copy.wait_send()
    for copy in k_x + v_x + q_x + g_x + k_z + v_z + flat(k_own + k_other + v_own + v_other) + tau_first + tau_second + tau_third:
        copy.wait_send()


def copy_out(*refs):
    n = (len(refs) - 2) // 3
    sources, results, held = refs[:n], refs[n : 2 * n], refs[2 * n : 3 * n]
    in_sem, out_sem = refs[3 * n :]
    pieces = [(i, m) for i in range(n) for m in range(OWN if i < n - 1 else 1)]

    def piece(ref, i, m):
        return ref.at[m] if i < n - 1 else ref

    into = [pltpu.make_async_copy(piece(sources[i], i, m), piece(held[i], i, m), in_sem.at[j]) for j, (i, m) in enumerate(pieces)]
    away = [pltpu.make_async_copy(piece(held[i], i, m), piece(results[i], i, m), out_sem.at[j]) for j, (i, m) in enumerate(pieces)]
    for copy in into:
        copy.start()
    for first, second in zip(into, away):
        first.wait()
        second.start()
    for copy in away:
        copy.wait()


def body(queries, keys, values, tau, out_grad, key_blocks):
    anywhere = pl.BlockSpec(memory_space=pl.ANY)
    scalars = pl.BlockSpec(memory_space=pltpu.SMEM)
    shape = lambda a: (OWN, BLOCK, a.shape[2])
    chunk = (CHUNK, BLOCK, HD)
    blocked = [a.reshape(shape(a)) for a in (queries, keys, values, out_grad)]
    outs = pl.pallas_call(
        kernel,
        name="attention",
        out_shape=(
            jax.ShapeDtypeStruct(shape(queries), bf16),
            jax.ShapeDtypeStruct(shape(queries), bf16),
            jax.ShapeDtypeStruct(shape(keys), bf16),
            jax.ShapeDtypeStruct(shape(keys), bf16),
            jax.ShapeDtypeStruct((HEADS,), f32),
        ),
        in_specs=[scalars, scalars] + [anywhere] * 4,
        out_specs=(anywhere,) * 4 + (scalars,),
        scratch_shapes=[
            pltpu.VMEM((WINDOW, BLOCK, HD), bf16),
            pltpu.VMEM((WINDOW, BLOCK, HD), bf16),
            pltpu.VMEM((ROWS, BLOCK, WIDE), bf16),
            pltpu.VMEM((ROWS, BLOCK, WIDE), bf16),
            pltpu.VMEM((ROWS, LISTED, BLOCK, WIDE), f32),
            pltpu.VMEM((ROWS, LISTED, BLOCK, WIDE), bf16),
            pltpu.VMEM((ROWS, 8, WIDE), f32),
            pltpu.VMEM((ROWS, 8, WIDE), f32),
            pltpu.VMEM((WINDOW, BLOCK, HD), f32),
            pltpu.VMEM((WINDOW, BLOCK, HD), f32),
            pltpu.VMEM((ROWS, 2, BLOCK, WIDE), bf16),
            pltpu.VMEM((8 * PARTS,) + chunk, bf16),
            pltpu.VMEM((8 * PARTS,) + chunk, bf16),
            pltpu.VMEM((2 * PARTS,) + chunk, bf16),
            pltpu.VMEM((2 * PARTS,) + chunk, bf16),
            pltpu.VMEM((2, HALF, BLOCK, HD), bf16),
            pltpu.VMEM((8, WIDE), f32),
            pltpu.VMEM((NX, 8, BLOCK), f32),
            pltpu.VMEM((NY, NX, 8, BLOCK), f32),
            pltpu.VMEM((NZ * BATCH, NX, 8, BLOCK), f32),
            pltpu.SemaphoreType.DMA((8,)),
            pltpu.SemaphoreType.DMA((24 + 2 * PARTS + 2 * len(PIECES),)),
            pltpu.SemaphoreType.DMA((24 + 2 * PARTS + 2 * len(PIECES),)),
            pltpu.SemaphoreType.DMA((2 * ROWS,)),
            pltpu.SemaphoreType.DMA((2 * ROWS,)),
            pltpu.SemaphoreType.DMA((2 * len(PIECES),)),
            pltpu.SemaphoreType.DMA((2 * len(PIECES),)),
            pltpu.SemaphoreType.DMA((2 * PARTS,)),
            pltpu.SemaphoreType.DMA((2 * PARTS,)),
            pltpu.SemaphoreType.DMA((2 * NX * OWN,)),
            pltpu.SemaphoreType.DMA((2 * NX * OWN,)),
            pltpu.SemaphoreType.DMA((13,)),
            pltpu.SemaphoreType.DMA((13,)),
        ],
        compiler_params=pltpu.CompilerParams(
            collective_id=0, has_side_effects=True, vmem_limit_bytes=62 << 20
        ),
    )(key_blocks.transpose(2, 0, 1), tau, *blocked)
    outs = pl.pallas_call(
        copy_out,
        name="copy_out",
        out_shape=tuple(jax.ShapeDtypeStruct(o.shape, o.dtype) for o in outs),
        in_specs=[anywhere] * len(outs),
        out_specs=(anywhere,) * len(outs),
        scratch_shapes=[pltpu.VMEM(o.shape, o.dtype) for o in outs] + [pltpu.SemaphoreType.DMA((9,))] * 2,
    )(*outs)
    return tuple(o.reshape(a.shape) for o, a in zip(outs[:4], (queries, queries, keys, keys))) + (outs[4],)


def solution(mesh):
    sharded = P("batch", "ctx", None)
    return jax.shard_map(
        body,
        mesh=mesh,
        in_specs=(sharded, sharded, sharded, P(), sharded, P()),
        out_specs=(sharded, sharded, sharded, sharded, P()),
        check_vma=False,
    )
```
